32 devices in a mesh: lat: 16 (over z, y, x), field: 2 (over core).
Axes of the slice: x: 2, y: 2, z: 4, core: 2. Of those that a mesh axis runs over, the one named last changes fastest.
Arguments:
- fields_grid: bfloat16 [2, 64, 2, 48, 192], P('field', None, None, 'lat'), may hold values from -6 to 6
- basis: bfloat16 [128, 48, 96], P('lat'), may hold values from -0.875 to 0.875
- order_table: int32 [16, 8], replicated, may hold values from -1 to 95, as said below
- panel_modes: int32 [2, 64], replicated, may hold values from 0 to 95, as said below
Outputs:
- panel: bfloat16 [2, 128, 192, 128], P('field', 'lat')
The draws below stay inside these ranges and needn't reach their ends.
Inputs may be any that keep to these rules, and one draw needn't show every extreme that they name: `order_table`: each order 0 to 95 stands in exactly one slot; every other slot holds -1; some group has all 8 slots filled. `panel_modes`: row 1 is never smaller than row 0 in the same column; degree 95 appears.
All inputs are finite; a program needn't handle non-finite values.
Results may differ from the reference program's by a relative error of at most 0.0082.
Values may be sent and summed in bfloat16 or wider, within the bound.
A program may use at most 64 MiB of HBM per device.

```python
import math
import jax
import jax.numpy as jnp
from jax import lax

SLOTS = 8
SNAP = 64
NMODE = 64
GROUPS = 16
NPAIR = 48
NLON = 192
NORD = 96
LDEG = 96


def draw_order_table(key, part):
    total = GROUPS * SLOTS
    first_key, second_key, third_key = jax.random.split(key, 3)
    full_group = jax.random.randint(first_key, (), 0, GROUPS)
    positions = jax.random.permutation(second_key, total)
    priority = jnp.where(positions // SLOTS == full_group, 0, 1).astype(jnp.int32)
    ordered = positions[jnp.argsort(priority, stable=True)]
    orders = jax.random.permutation(third_key, NORD).astype(jnp.int32)
    flat_table = jnp.full((total,), -1, dtype=jnp.int32).at[ordered[:NORD]].set(orders)
    return flat_table.reshape(GROUPS, SLOTS).astype(jnp.int32)


def draw_panel_modes(key, part):
    first_key, second_key = jax.random.split(key)
    mode_order = jax.random.randint(first_key, (NMODE,), 0, NORD).astype(jnp.int32)
    offset = jax.random.randint(second_key, (NMODE,), 0, LDEG - mode_order).astype(jnp.int32)
    degree = mode_order + offset
    mode_order = mode_order.at[0].set(0).at[1].set(NORD - 1)
    degree = degree.at[0].set(NORD - 1).at[1].set(NORD - 1)
    return jnp.stack([mode_order, degree]).astype(jnp.int32)


def levels(stream_key, extent, cuts, least, top_value):
    def one(axis_at, blocks):
        draws = jax.random.uniform(jax.random.fold_in(jax.random.fold_in(stream_key, 6), axis_at), (blocks,), jnp.float32, least / len(cuts), top_value / len(cuts))
        return jnp.repeat(jnp.exp(draws), extent[axis_at] // blocks).reshape((-1,) + (1,) * (len(extent) - axis_at - 1))

    gain = one(*cuts[0])
    for cut in cuts[1:]:
        gain = gain * one(*cut)
    return gain


def gaussian(stream_key, extent, width, bound, shards=(), kind=jnp.bfloat16):
    loudness = levels(stream_key, extent, shards, -0.22, 0.18) if shards else 1.0
    values = jax.random.normal(stream_key, extent, jnp.float32) * width * loudness
    return jnp.minimum(jnp.maximum(values, -bound), bound).astype(kind)


def setup_inputs(seed: int = 0) -> dict:
    keys = jax.random.split(jax.random.key(seed), 5)
    fields_grid = gaussian(keys[0], (2, SNAP, 2, NPAIR, NLON), 1.0, 6.0, ((0, 2), (3, 16)))
    basis = gaussian(keys[1], (GROUPS * SLOTS, NPAIR, LDEG), NPAIR ** -0.5, 0.875, ((0, 16),))
    order_table = draw_order_table(jax.random.fold_in(keys[4], 71), 0)
    panel_modes = draw_panel_modes(jax.random.fold_in(keys[4], 71), 0)
    return {"fields_grid": fields_grid, "basis": basis, "order_table": order_table, "panel_modes": panel_modes}


def dft_table(orders, lon_count):
    valid_slot = orders >= 0
    safe_orders = jnp.maximum(orders, 0).astype(jnp.int32)
    products = jnp.arange(lon_count, dtype=jnp.int32)[:, None] * safe_orders[None, :] % lon_count
    angles = products.astype(jnp.float32) * (2.0 * math.pi / lon_count)
    cosine = jnp.where(valid_slot[None, :], jnp.cos(angles), 0.0).astype(jnp.bfloat16)
    sine_table = jnp.where(valid_slot[None, :], -jnp.sin(angles), 0.0).astype(jnp.bfloat16)
    return jnp.stack([cosine, sine_table], axis=1)

def field_coefficients(grid_one, basis, orders, dft):
    snap_count = grid_one.shape[0]
    slot_all = orders.shape[0]
    fourier = jnp.einsum('thjn,nrk->hkjrt', grid_one, dft, preferred_element_type=jnp.float32) * (1.0 / math.sqrt(NLON))
    fourier = fourier.reshape(2, slot_all, NPAIR, 2 * snap_count)
    parity_parts = jnp.stack([fourier[0] + fourier[1], fourier[0] - fourier[1]]).astype(jnp.bfloat16)
    degree = jnp.arange(LDEG, dtype=jnp.int32)

    def one_group(index):
        start = (index * SLOTS).astype(jnp.int32)
        basis_block = lax.dynamic_slice_in_dim(basis, start, SLOTS, 0).astype(jnp.float32)
        even_block = lax.dynamic_slice_in_dim(parity_parts[0], start, SLOTS, 0).astype(jnp.float32)
        odd_block = lax.dynamic_slice_in_dim(parity_parts[1], start, SLOTS, 0).astype(jnp.float32)
        group_orders = lax.dynamic_slice_in_dim(orders, start, SLOTS, 0)
        even_product = jnp.einsum('sjl,sjc->slc', basis_block, even_block)
        odd_product = jnp.einsum('sjl,sjc->slc', basis_block, odd_block)
        parity_odd = (degree[None, :] - group_orders[:, None]) % 2 == 1
        chosen = jnp.where(parity_odd[:, :, None], odd_product, even_product)
        keep_mask = (degree[None, :] >= group_orders[:, None]) & (group_orders >= 0)[:, None]
        return jnp.where(keep_mask[:, :, None], chosen, 0.0).astype(jnp.bfloat16)
    blocks = lax.map(one_group, jnp.arange(slot_all // SLOTS, dtype=jnp.int32))
    return blocks.reshape(slot_all, LDEG, 2 * snap_count)

def reference(fields_grid, basis, order_table, panel_modes):
    snap_count = fields_grid.shape[1]
    orders = order_table.reshape(-1).astype(jnp.int32)
    slot_all = orders.shape[0]
    dft = dft_table(orders, NLON)
    coefficients = lax.map(lambda grid_one: field_coefficients(grid_one, basis, orders, dft), fields_grid)
    mode_order = panel_modes[0].astype(jnp.int32)
    mode_degree = panel_modes[1].astype(jnp.int32)
    slot_of_mode = jnp.argmax(orders[None, :] == mode_order[:, None], axis=1).astype(jnp.int32)
    mode_values = coefficients[:, slot_of_mode, mode_degree, :]
    columns = mode_values.astype(jnp.float32).reshape(2, NMODE * 2, snap_count)
    centered = (columns - lax.optimization_barrier(jnp.mean(columns, axis=2, keepdims=True))).astype(jnp.bfloat16)
    scale = 1.0 / (snap_count - 1)

    def one_field(index):
        own = coefficients[index]
        partner = centered[1 - index]

        def one_group(group):
            start = (group * SLOTS).astype(jnp.int32)
            block = lax.dynamic_slice_in_dim(own, start, SLOTS, 0).reshape(SLOTS * LDEG * 2, snap_count)
            values = jnp.dot(block, partner.T, preferred_element_type=jnp.float32) * scale
            return values.astype(jnp.bfloat16).reshape(SLOTS, 2 * LDEG, 2 * NMODE)
        return lax.map(one_group, jnp.arange(slot_all // SLOTS, dtype=jnp.int32)).reshape(slot_all, 2 * LDEG, 2 * NMODE)
    return lax.map(one_field, jnp.arange(2, dtype=jnp.int32))
```

```python
import functools
import math

import jax
import jax.numpy as jnp
import numpy as np
from jax import lax
from jax.experimental import pallas as pl
from jax.experimental.pallas import tpu as pltpu
from jax.sharding import PartitionSpec as P

BF = jnp.bfloat16
F32 = jnp.float32
NT = (((1,), (1,)), ((), ()))


def iota(shape, dim):
    return lax.broadcasted_iota(jnp.int32, shape, dim)


def mm(a, b):
    return jnp.dot(a, b, preferred_element_type=F32)


def mm_nt(a, b):
    return lax.dot_general(a, b, NT, preferred_element_type=F32)


def kernel(
    lat_count, snap, pairs, lon, slots, degs, first, owners, per,
    x_hbm, basis_hbm, table_hbm, orders_hbm, modes_hbm,
    coef_ref, twice_ref,
    x_ref, basis_ref, table_ref, orders_ref, modes_ref, load_sem,
    send, recv, tail_send, tail_recv, col_send, col_recv, mode_send, mode_recv, wide, rows,
    send_sem, recv_sem, tail_send_sem, tail_recv_sem, col_send_sem, col_recv_sem,
    mode_send_sem, mode_recv_sem, late,
):
    me = lax.axis_index("lat")
    field = lax.axis_index("field")
    other = 1 - field
    pair_total = lat_count * pairs
    width = 2 * snap
    block = 2 * slots
    slot_all = lat_count * slots
    modes = owners * per
    early = first + owners
    is_early = me < early
    in_owners = (me >= first) & (me < early)
    is_owner = in_owners & (field == 1)

    loads = [
        pltpu.make_async_copy(src, dst, load_sem.at[at])
        for at, (src, dst) in enumerate([
            (modes_hbm, modes_ref), (orders_hbm, orders_ref), (table_hbm, table_ref),
            (basis_hbm, basis_ref), (x_hbm, x_ref),
        ])
    ]
    for load in loads:
        load.start()

    barrier = pltpu.get_barrier_semaphore()

    def signal(sem, lat, core):
        pl.semaphore_signal(sem, inc=1, device_id=(lat, core), device_id_type=pl.DeviceIdType.MESH)

    def owns(lat):
        return (lat >= first) & (lat < early)

    def greet(lat, c):
        @pl.when((lat != me) & (is_early | (lat >= early)))
        def _():
            signal(barrier, lat, field)

        @pl.when(is_early & (is_owner | ((field == 0) & owns(lat))))
        def _():
            signal(barrier, lat, other)
        return c

    lax.fori_loop(0, lat_count, greet, 0)

    nord = table_ref.shape[0] // 2
    loads[0].wait()
    loads[1].wait()
    diagonal = iota((modes, modes), 0) == iota((modes, modes), 1)
    mode_col = jnp.sum(jnp.where(diagonal, modes_ref[0:1, :], 0), axis=1, keepdims=True)
    deg_col = jnp.sum(jnp.where(diagonal, modes_ref[1:2, :], 0), axis=1, keepdims=True)
    mode_odd = ((deg_col - mode_col) & 1) == 1
    by_slot = orders_ref[...]
    my_orders = jnp.sum(
        jnp.where(iota((slots, lat_count), 1) == me, by_slot, 0), axis=1, keepdims=True
    )

    def waves(cosine_row, sine_row):
        want = jnp.concatenate([cosine_row, sine_row], axis=0)
        onehot = (iota((want.shape[0], 2 * nord), 1) == want).astype(F32).astype(BF)
        return mm(onehot, table_ref[...]).astype(BF)

    loads[2].wait()
    mode_dft = waves(mode_col, mode_col + nord)
    loads[3].wait()
    cols = jnp.zeros((modes, pair_total), F32)
    at_degree = iota((modes, degs), 1) == deg_col
    for s in range(slots):
        pick = at_degree & (mode_col == my_orders[s:s + 1, :])
        cols = cols + mm_nt(pick.astype(F32).astype(BF), basis_ref[s])
    cols = jnp.concatenate([cols, jnp.zeros((modes, width - pair_total), F32)], axis=1)
    col_send[...] = cols.reshape(owners, per, width).astype(BF)
    even_lane = iota((1, width), 1) % 2 == 0

    def hemispheres(table, j):
        wave = mm_nt(table, x_ref[:, j].reshape(width, lon)) * (1.0 / math.sqrt(lon))
        half = wave.shape[0] // 2
        real, imag = wave[:half], wave[half:]
        north = jnp.where(even_lane, real, pltpu.roll(imag, 1, 1))
        south = jnp.where(even_lane, pltpu.roll(real, width - 1, 1), imag)
        return north, south

    loads[4].wait()
    for j in range(pairs):
        north, south = hemispheres(mode_dft, j)
        part = jnp.where(mode_odd, north - south, north + south)
        tail_send[:, j * per:(j + 1) * per, :] = part.reshape(owners, per, width).astype(BF)

    across = jnp.where(field == 0, owners, jnp.where(is_owner, early, 0))
    across_late = jnp.where(field == 0, owners, 0)
    pl.semaphore_wait(
        barrier, jnp.where(is_early, early - 1 + across, lat_count - 1 + across_late)
    )

    @pl.when(jnp.logical_not(is_early))
    def _():
        def arrive(lat, c):
            signal(late, lat, field)

            @pl.when((field == 0) & owns(lat))
            def _():
                signal(late, lat, other)
            return c

        lax.fori_loop(0, early, arrive, 0)

    def remote(src, dst, sems, lat, core):
        return pltpu.make_async_remote_copy(
            src_ref=src, dst_ref=dst, send_sem=sems[0], recv_sem=sems[1],
            device_id=(lat, core), device_id_type=pl.DeviceIdType.MESH,
        )

    block_sems = (send_sem, recv_sem)
    col_sems = (col_send_sem, col_recv_sem)

    def mode_sems(core):
        return (mode_send_sem.at[core], mode_recv_sem)

    def tail_sems(core):
        return (tail_send_sem, tail_recv_sem.at[core])

    def whole(ref, count, sems):
        part = ref.at[pl.ds(0, count)]
        return remote(part, part, sems, me, other)

    def start_tail(at, c):
        @pl.when((field == 1) & (at + first != me))
        def _():
            remote(col_send.at[at], col_recv.at[me], col_sems, at + first, 1).start()

        @pl.when((field == 0) | (at + first != me))
        def _():
            remote(tail_send.at[at], tail_recv.at[field, me], tail_sems(field), at + first, 1).start()
        return c

    lax.fori_loop(0, owners, start_tail, 0)

    tiled = jnp.concatenate([by_slot] * lat_count, axis=0)
    here = iota((slot_all, lat_count), 1) == iota((slot_all, lat_count), 0) // slots
    order_col = jnp.sum(jnp.where(here, tiled, 0), axis=1, keepdims=True)
    slot_dft = waves(order_col, jnp.where(order_col >= 0, order_col + nord, -1))
    for j in range(pairs):
        north, south = hemispheres(slot_dft, j)
        shape = (lat_count, slots, width)
        both = jnp.concatenate([(north + south).reshape(shape), (north - south).reshape(shape)], axis=1)
        send[:, j * block:(j + 1) * block, :] = both.astype(BF)

    def start_block(lat, c):
        @pl.when(lat != me)
        def _():
            remote(send.at[lat], recv.at[me], block_sems, lat, field).start()
        return c

    lax.fori_loop(0, first, start_block, 0)

    dup = (iota((2 * degs, degs), 0) // 2 == iota((2 * degs, degs), 1)).astype(F32).astype(BF)
    twin = (iota((pair_total, 2 * pair_total), 1) // 2 == iota((pair_total, 2 * pair_total), 0))
    twin = twin.astype(F32).astype(BF)
    deg = iota((2 * degs, 2 * pair_total), 0) // 2
    parity = iota((2 * degs, 2 * pair_total), 1) & 1
    for s in range(slots):
        order = my_orders[s:s + 1, :]
        base = mm(mm_nt(dup, basis_ref[s]).astype(BF), twin)
        keep = (deg >= order) & (order >= 0) & (((deg - order) & 1) == parity)
        rows[s] = jnp.where(keep, base, 0.0).astype(BF)

    lax.fori_loop(first, early, start_block, 0)

    @pl.when(is_early)
    def _():
        pl.semaphore_wait(late, (lat_count - early) * jnp.where(is_owner, 2, 1))

    lax.fori_loop(early, lat_count, start_block, 0)
    recv[me] = send[me]

    @pl.when(is_owner)
    def _():
        tail_recv[1, me] = tail_send[me - first]
        col_recv[me] = col_send[me - first]
        total = lat_count * pairs * per
        place = iota((width, total), 1)
        spread = iota((width, total), 0) == place // (pairs * per) * pairs + place // per % pairs
        own = iota((per, total), 0) == iota((per, total), 1) % per
        whole(col_recv, lat_count - 1, col_sems).wait_recv()
        column = jnp.sum(col_recv[...].astype(F32), axis=0).astype(BF)
        weights = jnp.where(own, mm(column, spread.astype(F32).astype(BF)), 0.0).astype(BF)

        def value_of(core):
            return mm(weights, tail_recv[core].reshape(total, width)).astype(BF)

        def start_mode(core):
            def start(lat, c):
                @pl.when((core == 0) | (lat != me))
                def _():
                    remote(
                        mode_send.at[1 - core], mode_recv.at[me - first], mode_sems(core), lat, core
                    ).start()
                return c

            lax.fori_loop(0, lat_count, start, 0)

        whole(tail_recv.at[1], lat_count - 1, tail_sems(1)).wait_recv()
        mode_send[1] = value_of(1)
        start_mode(0)
        whole(tail_recv.at[0], lat_count, tail_sems(0)).wait_recv()
        mode_send[0] = value_of(0)
        start_mode(1)
        mode_recv[me - first] = mode_send[0]

    whole(recv, lat_count - 1, block_sems).wait_recv()
    wide[...] = recv[...].reshape(slot_all * 2 * pairs, width).astype(F32)
    same_r = iota((2 * degs, width), 1) % 2 == iota((2 * degs, width), 0) % 2
    for s in range(slots):
        picked = wide[pl.ds(s, 2 * pair_total, stride=slots), :].astype(BF)
        coef_ref[s] = jnp.where(same_r, mm(rows[s], picked), 0.0).astype(BF)

    expand = (iota((2 * modes, modes), 1) == iota((2 * modes, modes), 0) // 2).astype(F32).astype(BF)
    u_match = iota((2 * modes, width), 1) % 2 == iota((2 * modes, width), 0) % 2
    row_even = iota((2 * modes, 1), 0) % 2 == 0

    @pl.when(is_owner)
    def _():
        whole(mode_recv, owners - 1, mode_sems(0)).wait_recv()

    @pl.when(jnp.logical_not(is_owner))
    def _():
        whole(mode_recv, owners, mode_sems(0)).wait_recv()

    columns = mm(expand, mode_recv[...].reshape(modes, width))
    masked = jnp.where(u_match, columns, 0.0)
    mean = jnp.sum(masked, axis=1, keepdims=True) * (1.0 / snap)
    centered = jnp.where(u_match, masked - mean, 0.0)
    moved = jnp.where(row_even, pltpu.roll(centered, 1, 1), pltpu.roll(centered, width - 1, 1))
    twice_ref[...] = (centered + moved).astype(BF)

    whole(send, lat_count - 1, block_sems).wait_send()

    @pl.when(is_owner)
    def _():
        whole(tail_send, owners - 1, tail_sems(field)).wait_send()
        whole(col_recv, lat_count, mode_sems(0)).wait_send()
        whole(col_recv, lat_count - 1, mode_sems(1)).wait_send()

    @pl.when(jnp.logical_not(is_owner))
    def _():
        whole(tail_send, owners, tail_sems(field)).wait_send()

    @pl.when((field == 1) & in_owners)
    def _():
        whole(col_send, owners - 1, col_sems).wait_send()

    @pl.when((field == 1) & jnp.logical_not(in_owners))
    def _():
        whole(col_send, owners, col_sems).wait_send()


def dft_constant(nord, lon):
    angles = (np.outer(np.arange(nord), np.arange(lon)) % lon) * (2.0 * math.pi / lon)
    return np.concatenate([np.cos(angles), -np.sin(angles)], axis=0).astype(np.float32).astype(BF)


def fused(lat_count, first, owners, fields_grid, basis, order_table, panel_modes):
    _, snap, _, pairs, lon = fields_grid.shape
    slots, pair_total, degs = basis.shape
    modes = panel_modes.shape[1]
    per = modes // owners
    width = 2 * snap
    block = 2 * slots
    head = pairs * block
    x = fields_grid[0].transpose(0, 2, 1, 3)
    table = jnp.asarray(dft_constant(degs, lon))
    vmem = pl.BlockSpec(memory_space=pltpu.VMEM)
    body = functools.partial(kernel, lat_count, snap, pairs, lon, slots, degs, first, owners, per)
    coef, twice = pl.pallas_call(
        body,
        out_shape=(
            jax.ShapeDtypeStruct((slots, 2 * degs, width), BF),
            jax.ShapeDtypeStruct((2 * modes, width), BF),
        ),
        in_specs=[pl.BlockSpec(memory_space=pl.ANY)] * 5,
        out_specs=(vmem, vmem),
        scratch_shapes=[
            pltpu.VMEM(x.shape, BF),
            pltpu.VMEM(basis.shape, BF),
            pltpu.VMEM(table.shape, BF),
            pltpu.VMEM((slots, lat_count), jnp.int32),
            pltpu.VMEM(panel_modes.shape, jnp.int32),
            pltpu.SemaphoreType.DMA((5,)),
            pltpu.VMEM((lat_count, head, width), BF),
            pltpu.VMEM((lat_count, head, width), BF),
            pltpu.VMEM((owners, pairs * per, width), BF),
            pltpu.VMEM((2, lat_count, pairs * per, width), BF),
            pltpu.VMEM((owners, per, width), BF),
            pltpu.VMEM((lat_count, per, width), BF),
            pltpu.VMEM((2, per, width), BF),
            pltpu.VMEM((owners, per, width), BF),
            pltpu.VMEM((lat_count * head, width), F32),
            pltpu.VMEM((slots, 2 * degs, 2 * pair_total), BF),
        ] + [pltpu.SemaphoreType.DMA] * 3 + [
            pltpu.SemaphoreType.DMA((2,)),
            pltpu.SemaphoreType.DMA,
            pltpu.SemaphoreType.DMA,
            pltpu.SemaphoreType.DMA((2,)),
            pltpu.SemaphoreType.DMA,
            pltpu.SemaphoreType.REGULAR,
        ],
        compiler_params=pltpu.CompilerParams(
            collective_id=0, has_side_effects=True, vmem_limit_bytes=52 * 1024 * 1024
        ),
    )(*[pltpu.with_memory_space_constraint(v, pltpu.HBM) for v in (x, basis, table, order_table.T, panel_modes)])
    panel = lax.dot_general(
        coef.reshape(slots * 2 * degs, width), twice, NT, preferred_element_type=F32
    ) * (1.0 / (snap - 1))
    return panel.astype(BF).reshape(1, slots, 2 * degs, 2 * modes)


def dft_table(orders, lon_count):
    valid_slot = orders >= 0
    safe_orders = jnp.maximum(orders, 0)
    products = lax.broadcasted_iota(jnp.int32, (lon_count, 1), 0) * safe_orders[None, :] % lon_count
    angles = products.astype(jnp.float32) * (2.0 * math.pi / lon_count)
    cosine = jnp.where(valid_slot[None, :], jnp.cos(angles), 0.0).astype(jnp.bfloat16)
    sine_table = jnp.where(valid_slot[None, :], -jnp.sin(angles), 0.0).astype(jnp.bfloat16)
    return jnp.stack([cosine, sine_table], axis=1)


def local(fields_grid, basis, order_table, panel_modes):
    grid_one = fields_grid[0]
    snap_count = grid_one.shape[0]
    pair_count = grid_one.shape[2]
    lon_count = grid_one.shape[3]
    slot_count = order_table.shape[1]
    deg_count = basis.shape[2]
    pair_total = basis.shape[1]
    mode_count = panel_modes.shape[1]
    orders = order_table.reshape(-1)
    slot_all = orders.shape[0]
    dft = dft_table(orders, lon_count)
    fourier = jnp.einsum("thjn,nrk->hkjrt", grid_one, dft, preferred_element_type=jnp.float32) * (
        1.0 / math.sqrt(lon_count)
    )
    fourier = fourier.reshape(2, slot_all, pair_count, 2 * snap_count)
    parity_parts = jnp.stack([fourier[0] + fourier[1], fourier[0] - fourier[1]]).astype(
        jnp.bfloat16
    )
    group_index = lax.axis_index("lat")
    my_orders = lax.dynamic_slice_in_dim(order_table, group_index, 1, 0)[0]
    my_odd = my_orders % 2 == 1
    basis_split = basis.reshape(slot_count, pair_total, deg_count // 2, 2)
    even_rows = basis_split[:, :, :, 0]
    odd_rows = basis_split[:, :, :, 1]
    degree = lax.broadcasted_iota(jnp.int32, (1, deg_count), 1)
    keep_mask = (degree >= my_orders[:, None]) & (my_orders >= 0)[:, None]
    received = lax.all_to_all(parity_parts, "lat", split_axis=1, concat_axis=2, tiled=True)
    first_parity = jnp.where(my_odd[:, None, None], received[1], received[0])
    second = jnp.where(my_odd[:, None, None], received[0], received[1])
    low_degrees = jnp.einsum(
        "sjh,sjc->shc", even_rows, first_parity, preferred_element_type=jnp.float32
    )
    high_degrees = jnp.einsum("sjh,sjc->shc", odd_rows, second, preferred_element_type=jnp.float32)
    joined = jnp.stack([low_degrees, high_degrees], axis=2).reshape(slot_count, deg_count, -1)
    coefficients = jnp.where(keep_mask[:, :, None], joined, 0.0).astype(jnp.bfloat16)
    mode_order = panel_modes[0]
    mode_degree = panel_modes[1]
    onehot = (my_orders[None, :] == mode_order[:, None]).astype(jnp.bfloat16)
    picked = jnp.take(coefficients, mode_degree, axis=1)
    local_values = jnp.einsum("ms,smc->mc", onehot, picked, preferred_element_type=jnp.float32)
    field_index = lax.axis_index("field")
    both_fields = jnp.stack(
        [
            jnp.where(field_index == 0, local_values, 0.0),
            jnp.where(field_index == 1, local_values, 0.0),
        ]
    )
    summed = lax.psum(both_fields, ("lat", "field"))
    other_field = jnp.where(field_index == 0, summed[1], summed[0]).astype(jnp.bfloat16)
    columns = other_field.astype(jnp.float32).reshape(mode_count * 2, snap_count)
    centered = (columns - jnp.mean(columns, axis=1, keepdims=True)).astype(jnp.bfloat16)
    coef_rows = coefficients.reshape(slot_count * deg_count * 2, snap_count)
    panel_values = lax.dot_general(
        coef_rows, centered, (((1,), (1,)), ((), ())), preferred_element_type=jnp.float32
    )
    panel_values = panel_values * (1.0 / (snap_count - 1))
    return panel_values.astype(jnp.bfloat16).reshape(1, slot_count, 2 * deg_count, 2 * mode_count)


def device_program(lat_count, fields_grid, basis, order_table, panel_modes):
    pairs, snap = fields_grid.shape[3], fields_grid.shape[1]
    slots, pair_total, degs = basis.shape
    modes = panel_modes.shape[1]
    first, owners = 1, lat_count // 2
    fits = (
        lat_count % 2 == 0
        and owners > first
        and modes % owners == 0
        and modes // owners == 8
        and 2 * snap == 128
        and slots == 8
        and degs <= 256
        and pair_total <= 2 * snap
        and lat_count * pairs * slots <= 512
    )
    if fits:
        return fused(lat_count, first, owners, fields_grid, basis, order_table, panel_modes)
    return local(fields_grid, basis, order_table, panel_modes)


def solution(mesh):
    placed = (P("field", None, None, "lat", None), P("lat", None, None), P(), P())
    return jax.shard_map(
        functools.partial(device_program, mesh.shape["lat"]),
        mesh=mesh, in_specs=placed, out_specs=P("field", "lat", None, None), check_vma=False,
    )
```

```python
import functools
import math

import jax
import jax.numpy as jnp
import numpy as np
from jax import lax
from jax.experimental import pallas as pl
from jax.experimental.pallas import tpu as pltpu
from jax.sharding import PartitionSpec as P

BF = jnp.bfloat16
F32 = jnp.float32
NT = (((1,), (1,)), ((), ()))


def iota(shape, dim):
    return lax.broadcasted_iota(jnp.int32, shape, dim)


def mm(a, b):
    return jnp.dot(a, b, preferred_element_type=F32)


def mm_nt(a, b):
    return lax.dot_general(a, b, NT, preferred_element_type=F32)


def kernel(
    lat_count, snap, pairs, lon, slots, degs, first, owners, per,
    x_hbm, basis_hbm, table_hbm, orders_hbm, modes_hbm,
    coef_ref, twice_ref,
    x_ref, basis_ref, table_ref, orders_ref, modes_ref, load_sem,
    send, recv, tail_send, tail_recv, col_send, col_recv, mode_send, mode_recv, wide, rows,
    send_sem, recv_sem, tail_send_sem, tail_recv_sem, col_send_sem, col_recv_sem,
    mode_send_sem, mode_recv_sem, late,
):
    me = lax.axis_index("lat")
    field = lax.axis_index("field")
    other = 1 - field
    pair_total = lat_count * pairs
    width = 2 * snap
    block = 2 * slots
    slot_all = lat_count * slots
    modes = owners * per
    early = first + owners
    is_early = me < early
    in_owners = (me >= first) & (me < early)
    is_owner = in_owners & (field == 1)

    loads = [
        pltpu.make_async_copy(src, dst, load_sem.at[at])
        for at, (src, dst) in enumerate([
            (table_hbm, table_ref), (modes_hbm, modes_ref), (orders_hbm, orders_ref),
            (basis_hbm, basis_ref), (x_hbm, x_ref),
        ])
    ]
    for load in loads:
        load.start()

    barrier = pltpu.get_barrier_semaphore()

    def signal(sem, lat, core):
        pl.semaphore_signal(sem, inc=1, device_id=(lat, core), device_id_type=pl.DeviceIdType.MESH)

    def owns(lat):
        return (lat >= first) & (lat < early)

    def greet(lat, c):
        @pl.when((lat != me) & (is_early | (lat >= early)))
        def _():
            signal(barrier, lat, field)

        @pl.when(is_early & (is_owner | ((field == 0) & owns(lat))))
        def _():
            signal(barrier, lat, other)
        return c

    lax.fori_loop(0, lat_count, greet, 0)

    nord = table_ref.shape[0] // 2
    loads[1].wait()
    loads[2].wait()
    diagonal = iota((modes, modes), 0) == iota((modes, modes), 1)
    mode_col = jnp.sum(jnp.where(diagonal, modes_ref[0:1, :], 0), axis=1, keepdims=True)
    deg_col = jnp.sum(jnp.where(diagonal, modes_ref[1:2, :], 0), axis=1, keepdims=True)
    mode_odd = ((deg_col - mode_col) & 1) == 1
    by_slot = orders_ref[...]
    my_orders = jnp.sum(
        jnp.where(iota((slots, lat_count), 1) == me, by_slot, 0), axis=1, keepdims=True
    )

    def waves(cosine_row, sine_row):
        want = jnp.concatenate([cosine_row, sine_row], axis=0)
        onehot = (iota((want.shape[0], 2 * nord), 1) == want).astype(F32).astype(BF)
        return mm(onehot, table_ref[...]).astype(BF)

    loads[0].wait()
    mode_dft = waves(mode_col, mode_col + nord)
    loads[3].wait()
    cols = jnp.zeros((modes, pair_total), F32)
    at_degree = iota((modes, degs), 1) == deg_col
    for s in range(slots):
        pick = at_degree & (mode_col == my_orders[s:s + 1, :])
        cols = cols + mm_nt(pick.astype(F32).astype(BF), basis_ref[s])
    cols = jnp.concatenate([cols, jnp.zeros((modes, width - pair_total), F32)], axis=1)
    col_send[...] = cols.reshape(owners, per, width).astype(BF)
    even_lane = iota((1, width), 1) % 2 == 0

    def hemispheres(table, j):
        wave = mm_nt(table, x_ref[:, j].reshape(width, lon)) * (1.0 / math.sqrt(lon))
        half = wave.shape[0] // 2
        real, imag = wave[:half], wave[half:]
        north = jnp.where(even_lane, real, pltpu.roll(imag, 1, 1))
        south = jnp.where(even_lane, pltpu.roll(real, width - 1, 1), imag)
        return north, south

    loads[4].wait()
    for j in range(pairs):
        north, south = hemispheres(mode_dft, j)
        part = jnp.where(mode_odd, north - south, north + south)
        tail_send[:, j * per:(j + 1) * per, :] = part.reshape(owners, per, width).astype(BF)

    across = jnp.where(field == 0, owners, jnp.where(is_owner, early, 0))
    across_late = jnp.where(field == 0, owners, 0)
    pl.semaphore_wait(
        barrier, jnp.where(is_early, early - 1 + across, lat_count - 1 + across_late)
    )

    def remote(src, dst, sems, lat, core):
        return pltpu.make_async_remote_copy(
            src_ref=src, dst_ref=dst, send_sem=sems[0], recv_sem=sems[1],
            device_id=(lat, core), device_id_type=pl.DeviceIdType.MESH,
        )

    block_sems = (send_sem, recv_sem)
    col_sems = (col_send_sem, col_recv_sem)

    def mode_sems(core):
        return (mode_send_sem.at[core], mode_recv_sem)

    def tail_sems(core):
        return (tail_send_sem, tail_recv_sem.at[core])

    def whole(ref, count, sems):
        part = ref.at[pl.ds(0, count)]
        return remote(part, part, sems, me, other)

    def start_tail(at, c):
        @pl.when((field == 1) & (at + first != me))
        def _():
            remote(col_send.at[at], col_recv.at[me], col_sems, at + first, 1).start()

        @pl.when((field == 0) | (at + first != me))
        def _():
            remote(tail_send.at[at], tail_recv.at[field, me], tail_sems(field), at + first, 1).start()
        return c

    lax.fori_loop(0, owners, start_tail, 0)

    @pl.when(jnp.logical_not(is_early))
    def _():
        def arrive(lat, c):
            signal(late, lat, field)

            @pl.when((field == 0) & owns(lat))
            def _():
                signal(late, lat, other)
            return c

        lax.fori_loop(0, early, arrive, 0)

    tiled = jnp.concatenate([by_slot] * lat_count, axis=0)
    here = iota((slot_all, lat_count), 1) == iota((slot_all, lat_count), 0) // slots
    order_col = jnp.sum(jnp.where(here, tiled, 0), axis=1, keepdims=True)
    slot_dft = waves(order_col, jnp.where(order_col >= 0, order_col + nord, -1))
    for j in range(pairs):
        north, south = hemispheres(slot_dft, j)
        shape = (lat_count, slots, width)
        both = jnp.concatenate([(north + south).reshape(shape), (north - south).reshape(shape)], axis=1)
        send[:, j * block:(j + 1) * block, :] = both.astype(BF)

    def start_block(lat, c):
        @pl.when(lat != me)
        def _():
            remote(send.at[lat], recv.at[me], block_sems, lat, field).start()
        return c

    lax.fori_loop(0, 1, start_block, 0)

    dup = (iota((2 * degs, degs), 0) // 2 == iota((2 * degs, degs), 1)).astype(F32).astype(BF)
    twin = (iota((pair_total, 2 * pair_total), 1) // 2 == iota((pair_total, 2 * pair_total), 0))
    twin = twin.astype(F32).astype(BF)
    deg = iota((2 * degs, 2 * pair_total), 0) // 2
    parity = iota((2 * degs, 2 * pair_total), 1) & 1
    for s in range(slots):
        order = my_orders[s:s + 1, :]
        base = mm(mm_nt(dup, basis_ref[s]).astype(BF), twin)
        keep = (deg >= order) & (order >= 0) & (((deg - order) & 1) == parity)
        rows[s] = jnp.where(keep, base, 0.0).astype(BF)

    @pl.when(jnp.logical_not(is_owner))
    def _():
        lax.fori_loop(1, early, start_block, 0)

    @pl.when(is_early)
    def _():
        pl.semaphore_wait(late, (lat_count - early) * jnp.where(is_owner, 2, 1))

    lax.fori_loop(early, lat_count, start_block, 0)
    recv[me] = send[me]

    @pl.when(is_owner)
    def _():
        tail_recv[1, me] = tail_send[me - first]
        col_recv[me] = col_send[me - first]
        total = lat_count * pairs * per
        place = iota((width, total), 1)
        spread = iota((width, total), 0) == place // (pairs * per) * pairs + place // per % pairs
        own = iota((per, total), 0) == iota((per, total), 1) % per
        whole(col_recv, lat_count - 1, col_sems).wait_recv()
        column = jnp.sum(col_recv[...].astype(F32), axis=0).astype(BF)
        weights = jnp.where(own, mm(column, spread.astype(F32).astype(BF)), 0.0).astype(BF)

        def value_of(core):
            return mm(weights, tail_recv[core].reshape(total, width)).astype(BF)

        def start_mode(core):
            def start(lat, c):
                @pl.when((core == 0) | (lat != me))
                def _():
                    remote(
                        mode_send.at[1 - core], mode_recv.at[me - first], mode_sems(core), lat, core
                    ).start()
                return c

            lax.fori_loop(0, lat_count, start, 0)

        whole(tail_recv.at[1], lat_count - 1, tail_sems(1)).wait_recv()
        mode_send[1] = value_of(1)
        start_mode(0)
        whole(tail_recv.at[0], lat_count, tail_sems(0)).wait_recv()
        mode_send[0] = value_of(0)
        start_mode(1)
        lax.fori_loop(1, early, start_block, 0)
        mode_recv[me - first] = mode_send[0]

    whole(recv, lat_count - 1, block_sems).wait_recv()
    wide[...] = recv[...].reshape(slot_all * 2 * pairs, width).astype(F32)
    same_r = iota((2 * degs, width), 1) % 2 == iota((2 * degs, width), 0) % 2
    for s in range(slots):
        picked = wide[pl.ds(s, 2 * pair_total, stride=slots), :].astype(BF)
        coef_ref[s] = jnp.where(same_r, mm(rows[s], picked), 0.0).astype(BF)

    expand = (iota((2 * modes, modes), 1) == iota((2 * modes, modes), 0) // 2).astype(F32).astype(BF)
    u_match = iota((2 * modes, width), 1) % 2 == iota((2 * modes, width), 0) % 2
    row_even = iota((2 * modes, 1), 0) % 2 == 0

    @pl.when(is_owner)
    def _():
        whole(mode_recv, owners - 1, mode_sems(0)).wait_recv()

    @pl.when(jnp.logical_not(is_owner))
    def _():
        whole(mode_recv, owners, mode_sems(0)).wait_recv()

    columns = mm(expand, mode_recv[...].reshape(modes, width))
    masked = jnp.where(u_match, columns, 0.0)
    mean = jnp.sum(masked, axis=1, keepdims=True) * (1.0 / snap)
    centered = jnp.where(u_match, masked - mean, 0.0)
    moved = jnp.where(row_even, pltpu.roll(centered, 1, 1), pltpu.roll(centered, width - 1, 1))
    twice_ref[...] = (centered + moved).astype(BF)

    whole(send, lat_count - 1, block_sems).wait_send()

    @pl.when(is_owner)
    def _():
        whole(tail_send, owners - 1, tail_sems(field)).wait_send()
        whole(col_recv, lat_count, mode_sems(0)).wait_send()
        whole(col_recv, lat_count - 1, mode_sems(1)).wait_send()

    @pl.when(jnp.logical_not(is_owner))
    def _():
        whole(tail_send, owners, tail_sems(field)).wait_send()

    @pl.when((field == 1) & in_owners)
    def _():
        whole(col_send, owners - 1, col_sems).wait_send()

    @pl.when((field == 1) & jnp.logical_not(in_owners))
    def _():
        whole(col_send, owners, col_sems).wait_send()


def dft_constant(nord, lon):
    angles = (np.outer(np.arange(nord), np.arange(lon)) % lon) * (2.0 * math.pi / lon)
    return np.concatenate([np.cos(angles), -np.sin(angles)], axis=0).astype(np.float32).astype(BF)


def fused(lat_count, first, owners, fields_grid, basis, order_table, panel_modes):
    _, snap, _, pairs, lon = fields_grid.shape
    slots, pair_total, degs = basis.shape
    modes = panel_modes.shape[1]
    per = modes // owners
    width = 2 * snap
    block = 2 * slots
    head = pairs * block
    x = fields_grid[0].transpose(0, 2, 1, 3)
    table = jnp.asarray(dft_constant(degs, lon))
    vmem = pl.BlockSpec(memory_space=pltpu.VMEM)
    body = functools.partial(kernel, lat_count, snap, pairs, lon, slots, degs, first, owners, per)
    coef, twice = pl.pallas_call(
        body,
        out_shape=(
            jax.ShapeDtypeStruct((slots, 2 * degs, width), BF),
            jax.ShapeDtypeStruct((2 * modes, width), BF),
        ),
        in_specs=[pl.BlockSpec(memory_space=pl.ANY)] * 5,
        out_specs=(vmem, vmem),
        scratch_shapes=[
            pltpu.VMEM(x.shape, BF),
            pltpu.VMEM(basis.shape, BF),
            pltpu.VMEM(table.shape, BF),
            pltpu.VMEM((slots, lat_count), jnp.int32),
            pltpu.VMEM(panel_modes.shape, jnp.int32),
            pltpu.SemaphoreType.DMA((5,)),
            pltpu.VMEM((lat_count, head, width), BF),
            pltpu.VMEM((lat_count, head, width), BF),
            pltpu.VMEM((owners, pairs * per, width), BF),
            pltpu.VMEM((2, lat_count, pairs * per, width), BF),
            pltpu.VMEM((owners, per, width), BF),
            pltpu.VMEM((lat_count, per, width), BF),
            pltpu.VMEM((2, per, width), BF),
            pltpu.VMEM((owners, per, width), BF),
            pltpu.VMEM((lat_count * head, width), F32),
            pltpu.VMEM((slots, 2 * degs, 2 * pair_total), BF),
        ] + [pltpu.SemaphoreType.DMA] * 3 + [
            pltpu.SemaphoreType.DMA((2,)),
            pltpu.SemaphoreType.DMA,
            pltpu.SemaphoreType.DMA,
            pltpu.SemaphoreType.DMA((2,)),
            pltpu.SemaphoreType.DMA,
            pltpu.SemaphoreType.REGULAR,
        ],
        compiler_params=pltpu.CompilerParams(
            collective_id=0, has_side_effects=True, vmem_limit_bytes=52 * 1024 * 1024
        ),
    )(*[pltpu.with_memory_space_constraint(v, pltpu.HBM) for v in (x, basis, table, order_table.T, panel_modes)])
    panel = lax.dot_general(
        coef.reshape(slots * 2 * degs, width), twice, NT, preferred_element_type=F32
    ) * (1.0 / (snap - 1))
    return panel.astype(BF).reshape(1, slots, 2 * degs, 2 * modes)


def dft_table(orders, lon_count):
    valid_slot = orders >= 0
    safe_orders = jnp.maximum(orders, 0)
    products = lax.broadcasted_iota(jnp.int32, (lon_count, 1), 0) * safe_orders[None, :] % lon_count
    angles = products.astype(jnp.float32) * (2.0 * math.pi / lon_count)
    cosine = jnp.where(valid_slot[None, :], jnp.cos(angles), 0.0).astype(jnp.bfloat16)
    sine_table = jnp.where(valid_slot[None, :], -jnp.sin(angles), 0.0).astype(jnp.bfloat16)
    return jnp.stack([cosine, sine_table], axis=1)


def local(fields_grid, basis, order_table, panel_modes):
    grid_one = fields_grid[0]
    snap_count = grid_one.shape[0]
    pair_count = grid_one.shape[2]
    lon_count = grid_one.shape[3]
    slot_count = order_table.shape[1]
    deg_count = basis.shape[2]
    pair_total = basis.shape[1]
    mode_count = panel_modes.shape[1]
    orders = order_table.reshape(-1)
    slot_all = orders.shape[0]
    dft = dft_table(orders, lon_count)
    fourier = jnp.einsum("thjn,nrk->hkjrt", grid_one, dft, preferred_element_type=jnp.float32) * (
        1.0 / math.sqrt(lon_count)
    )
    fourier = fourier.reshape(2, slot_all, pair_count, 2 * snap_count)
    parity_parts = jnp.stack([fourier[0] + fourier[1], fourier[0] - fourier[1]]).astype(
        jnp.bfloat16
    )
    group_index = lax.axis_index("lat")
    my_orders = lax.dynamic_slice_in_dim(order_table, group_index, 1, 0)[0]
    my_odd = my_orders % 2 == 1
    basis_split = basis.reshape(slot_count, pair_total, deg_count // 2, 2)
    even_rows = basis_split[:, :, :, 0]
    odd_rows = basis_split[:, :, :, 1]
    degree = lax.broadcasted_iota(jnp.int32, (1, deg_count), 1)
    keep_mask = (degree >= my_orders[:, None]) & (my_orders >= 0)[:, None]
    received = lax.all_to_all(parity_parts, "lat", split_axis=1, concat_axis=2, tiled=True)
    first_parity = jnp.where(my_odd[:, None, None], received[1], received[0])
    second = jnp.where(my_odd[:, None, None], received[0], received[1])
    low_degrees = jnp.einsum(
        "sjh,sjc->shc", even_rows, first_parity, preferred_element_type=jnp.float32
    )
    high_degrees = jnp.einsum("sjh,sjc->shc", odd_rows, second, preferred_element_type=jnp.float32)
    joined = jnp.stack([low_degrees, high_degrees], axis=2).reshape(slot_count, deg_count, -1)
    coefficients = jnp.where(keep_mask[:, :, None], joined, 0.0).astype(jnp.bfloat16)
    mode_order = panel_modes[0]
    mode_degree = panel_modes[1]
    onehot = (my_orders[None, :] == mode_order[:, None]).astype(jnp.bfloat16)
    picked = jnp.take(coefficients, mode_degree, axis=1)
    local_values = jnp.einsum("ms,smc->mc", onehot, picked, preferred_element_type=jnp.float32)
    field_index = lax.axis_index("field")
    both_fields = jnp.stack(
        [
            jnp.where(field_index == 0, local_values, 0.0),
            jnp.where(field_index == 1, local_values, 0.0),
        ]
    )
    summed = lax.psum(both_fields, ("lat", "field"))
    other_field = jnp.where(field_index == 0, summed[1], summed[0]).astype(jnp.bfloat16)
    columns = other_field.astype(jnp.float32).reshape(mode_count * 2, snap_count)
    centered = (columns - jnp.mean(columns, axis=1, keepdims=True)).astype(jnp.bfloat16)
    coef_rows = coefficients.reshape(slot_count * deg_count * 2, snap_count)
    panel_values = lax.dot_general(
        coef_rows, centered, (((1,), (1,)), ((), ())), preferred_element_type=jnp.float32
    )
    panel_values = panel_values * (1.0 / (snap_count - 1))
    return panel_values.astype(jnp.bfloat16).reshape(1, slot_count, 2 * deg_count, 2 * mode_count)


def device_program(lat_count, fields_grid, basis, order_table, panel_modes):
    pairs, snap = fields_grid.shape[3], fields_grid.shape[1]
    slots, pair_total, degs = basis.shape
    modes = panel_modes.shape[1]
    first, owners = 3, lat_count // 2
    fits = (
        lat_count % 2 == 0
        and owners > first
        and modes % owners == 0
        and modes // owners == 8
        and 2 * snap == 128
        and slots == 8
        and degs <= 256
        and pair_total <= 2 * snap
        and lat_count * pairs * slots <= 512
    )
    if fits:
        return fused(lat_count, first, owners, fields_grid, basis, order_table, panel_modes)
    return local(fields_grid, basis, order_table, panel_modes)


def solution(mesh):
    placed = (P("field", None, None, "lat", None), P("lat", None, None), P(), P())
    return jax.shard_map(
        functools.partial(device_program, mesh.shape["lat"]),
        mesh=mesh, in_specs=placed, out_specs=P("field", "lat", None, None), check_vma=False,
    )
```

```python
import functools
import math

import jax
import jax.numpy as jnp
import numpy as np
from jax import lax
from jax.experimental import pallas as pl
from jax.experimental.pallas import tpu as pltpu
from jax.sharding import PartitionSpec as P

BF = jnp.bfloat16
F32 = jnp.float32
NT = (((1,), (1,)), ((), ()))


def iota(shape, dim):
    return lax.broadcasted_iota(jnp.int32, shape, dim)


def mm(a, b):
    return jnp.dot(a, b, preferred_element_type=F32)


def mm_nt(a, b):
    return lax.dot_general(a, b, NT, preferred_element_type=F32)


def kernel(
    lat_count, snap, pairs, lon, slots, degs, first, owners, per,
    x_hbm, basis_hbm, table_hbm, orders_hbm, modes_hbm,
    coef_ref, twice_ref,
    x_ref, basis_ref, table_ref, orders_ref, modes_ref, load_sem,
    send, recv, tail_send, tail_recv, col_send, col_recv, mode_send, mode_recv, wide, rows,
    send_sem, recv_sem, tail_send_sem, tail_recv_sem, col_send_sem, col_recv_sem,
    mode_send_sem, mode_recv_sem, late,
):
    me = lax.axis_index("lat")
    field = lax.axis_index("field")
    other = 1 - field
    pair_total = lat_count * pairs
    width = 2 * snap
    block = 2 * slots
    slot_all = lat_count * slots
    modes = owners * per
    early = first + owners
    plane = lat_count // 4
    inner = me // plane * plane
    is_early = me < early
    in_owners = (me >= first) & (me < early)
    is_owner = in_owners & (field == 1)

    loads = [
        pltpu.make_async_copy(src, dst, load_sem.at[at])
        for at, (src, dst) in enumerate([
            (table_hbm, table_ref), (modes_hbm, modes_ref), (orders_hbm, orders_ref),
            (basis_hbm, basis_ref), (x_hbm, x_ref),
        ])
    ]
    for load in loads:
        load.start()

    barrier = pltpu.get_barrier_semaphore()

    def signal(sem, lat, core):
        pl.semaphore_signal(sem, inc=1, device_id=(lat, core), device_id_type=pl.DeviceIdType.MESH)

    def owns(lat):
        return (lat >= first) & (lat < early)

    def greet(lat, c):
        @pl.when((lat != me) & (is_early | (lat >= early)))
        def _():
            signal(barrier, lat, field)

        @pl.when(is_early & (is_owner | ((field == 0) & owns(lat))))
        def _():
            signal(barrier, lat, other)
        return c

    lax.fori_loop(0, lat_count, greet, 0)

    nord = table_ref.shape[0] // 2
    loads[1].wait()
    loads[2].wait()
    diagonal = iota((modes, modes), 0) == iota((modes, modes), 1)
    mode_col = jnp.sum(jnp.where(diagonal, modes_ref[0:1, :], 0), axis=1, keepdims=True)
    deg_col = jnp.sum(jnp.where(diagonal, modes_ref[1:2, :], 0), axis=1, keepdims=True)
    mode_odd = ((deg_col - mode_col) & 1) == 1
    by_slot = orders_ref[...]
    my_orders = jnp.sum(
        jnp.where(iota((slots, lat_count), 1) == me, by_slot, 0), axis=1, keepdims=True
    )

    def waves(cosine_row, sine_row):
        want = jnp.concatenate([cosine_row, sine_row], axis=0)
        onehot = (iota((want.shape[0], 2 * nord), 1) == want).astype(F32).astype(BF)
        return mm(onehot, table_ref[...]).astype(BF)

    loads[0].wait()
    mode_dft = waves(mode_col, mode_col + nord)
    even_lane = iota((1, width), 1) % 2 == 0

    def hemispheres(table, j):
        wave = mm_nt(table, x_ref[:, j].reshape(width, lon)) * (1.0 / math.sqrt(lon))
        half = wave.shape[0] // 2
        real, imag = wave[:half], wave[half:]
        north = jnp.where(even_lane, real, pltpu.roll(imag, 1, 1))
        south = jnp.where(even_lane, pltpu.roll(real, width - 1, 1), imag)
        return north, south

    loads[4].wait()
    for j in range(pairs):
        north, south = hemispheres(mode_dft, j)
        part = jnp.where(mode_odd, north - south, north + south)
        tail_send[:, j * per:(j + 1) * per, :] = part.reshape(owners, per, width).astype(BF)

    across = jnp.where(field == 0, owners, jnp.where(is_owner, early, 0))
    across_late = jnp.where(field == 0, owners, 0)
    pl.semaphore_wait(
        barrier, jnp.where(is_early, early - 1 + across, lat_count - 1 + across_late)
    )

    def remote(src, dst, sems, lat, core):
        return pltpu.make_async_remote_copy(
            src_ref=src, dst_ref=dst, send_sem=sems[0], recv_sem=sems[1],
            device_id=(lat, core), device_id_type=pl.DeviceIdType.MESH,
        )

    block_sems = (send_sem, recv_sem)
    col_sems = (col_send_sem, col_recv_sem)

    def mode_sems(core):
        return (mode_send_sem.at[core], mode_recv_sem)

    def tail_sems(core):
        return (tail_send_sem, tail_recv_sem.at[core])

    def whole(ref, count, sems):
        part = ref.at[pl.ds(0, count)]
        return remote(part, part, sems, me, other)

    def start_tail(at, c):
        @pl.when((field == 0) | (at + first != me))
        def _():
            remote(tail_send.at[at], tail_recv.at[field, me], tail_sems(field), at + first, 1).start()
        return c

    lax.fori_loop(0, owners, start_tail, 0)
    loads[3].wait()

    @pl.when(field == 1)
    def _():
        cols = jnp.zeros((modes, pair_total), F32)
        at_degree = iota((modes, degs), 1) == deg_col
        for s in range(slots):
            pick = at_degree & (mode_col == my_orders[s:s + 1, :])
            cols = cols + mm_nt(pick.astype(F32).astype(BF), basis_ref[s])
        cols = jnp.concatenate([cols, jnp.zeros((modes, width - pair_total), F32)], axis=1)
        col_send[...] = cols.reshape(owners, per, width).astype(BF)

        def start_col(at, c):
            @pl.when(at + first != me)
            def _():
                remote(col_send.at[at], col_recv.at[me], col_sems, at + first, 1).start()
            return c

        lax.fori_loop(0, owners, start_col, 0)

    @pl.when(jnp.logical_not(is_early))
    def _():
        def arrive(lat, c):
            signal(late, lat, field)

            @pl.when((field == 0) & owns(lat))
            def _():
                signal(late, lat, other)
            return c

        lax.fori_loop(0, early, arrive, 0)

    tiled = jnp.concatenate([by_slot] * lat_count, axis=0)
    here = iota((slot_all, lat_count), 1) == iota((slot_all, lat_count), 0) // slots
    order_col = jnp.sum(jnp.where(here, tiled, 0), axis=1, keepdims=True)
    slot_dft = waves(order_col, jnp.where(order_col >= 0, order_col + nord, -1))
    for j in range(pairs):
        north, south = hemispheres(slot_dft, j)
        shape = (lat_count, slots, width)
        both = jnp.concatenate([(north + south).reshape(shape), (north - south).reshape(shape)], axis=1)
        send[:, j * block:(j + 1) * block, :] = both.astype(BF)

    def start_block(lat, c):
        @pl.when(lat != me)
        def _():
            remote(send.at[lat], recv.at[me], block_sems, lat, field).start()
        return c

    lax.fori_loop(0, 1, start_block, 0)

    dup = (iota((2 * degs, degs), 0) // 2 == iota((2 * degs, degs), 1)).astype(F32).astype(BF)
    twin = (iota((pair_total, 2 * pair_total), 1) // 2 == iota((pair_total, 2 * pair_total), 0))
    twin = twin.astype(F32).astype(BF)
    deg = iota((2 * degs, 2 * pair_total), 0) // 2
    parity = iota((2 * degs, 2 * pair_total), 1) & 1
    for s in range(slots):
        order = my_orders[s:s + 1, :]
        base = mm(mm_nt(dup, basis_ref[s]).astype(BF), twin)
        keep = (deg >= order) & (order >= 0) & (((deg - order) & 1) == parity)
        rows[s] = jnp.where(keep, base, 0.0).astype(BF)

    lax.fori_loop(jnp.maximum(inner, 1), early, start_block, 0)

    @pl.when(me < lat_count // 2)
    def _():
        lax.fori_loop(1, jnp.minimum(inner, early), start_block, 0)

    @pl.when(is_early)
    def _():
        pl.semaphore_wait(late, (lat_count - early) * jnp.where(is_owner, 2, 1))

    lax.fori_loop(early, lat_count, start_block, 0)

    @pl.when(jnp.logical_not(is_owner) & (me >= lat_count // 2))
    def _():
        lax.fori_loop(1, jnp.minimum(inner, early), start_block, 0)

    recv[me] = send[me]

    @pl.when(is_owner)
    def _():
        tail_recv[1, me] = tail_send[me - first]
        col_recv[me] = col_send[me - first]
        total = lat_count * pairs * per
        place = iota((width, total), 1)
        spread = iota((width, total), 0) == place // (pairs * per) * pairs + place // per % pairs
        own = iota((per, total), 0) == iota((per, total), 1) % per
        whole(col_recv, lat_count - 1, col_sems).wait_recv()
        column = jnp.sum(col_recv[...].astype(F32), axis=0).astype(BF)
        weights = jnp.where(own, mm(column, spread.astype(F32).astype(BF)), 0.0).astype(BF)

        def value_of(core):
            return mm(weights, tail_recv[core].reshape(total, width)).astype(BF)

        def start_mode(core):
            def start(lat, c):
                @pl.when((core == 0) | (lat != me))
                def _():
                    remote(
                        mode_send.at[1 - core], mode_recv.at[me - first], mode_sems(core), lat, core
                    ).start()
                return c

            lax.fori_loop(0, lat_count, start, 0)

        whole(tail_recv.at[1], lat_count - 1, tail_sems(1)).wait_recv()
        mode_send[1] = value_of(1)
        start_mode(0)
        whole(tail_recv.at[0], lat_count, tail_sems(0)).wait_recv()
        mode_send[0] = value_of(0)
        start_mode(1)

        @pl.when(me >= lat_count // 2)
        def _():
            lax.fori_loop(1, jnp.minimum(inner, early), start_block, 0)

        mode_recv[me - first] = mode_send[0]

    whole(recv, lat_count - 1, block_sems).wait_recv()
    wide[...] = recv[...].reshape(slot_all * 2 * pairs, width).astype(F32)
    same_r = iota((2 * degs, width), 1) % 2 == iota((2 * degs, width), 0) % 2
    for s in range(slots):
        picked = wide[pl.ds(s, 2 * pair_total, stride=slots), :].astype(BF)
        coef_ref[s] = jnp.where(same_r, mm(rows[s], picked), 0.0).astype(BF)

    expand = (iota((2 * modes, modes), 1) == iota((2 * modes, modes), 0) // 2).astype(F32).astype(BF)
    u_match = iota((2 * modes, width), 1) % 2 == iota((2 * modes, width), 0) % 2
    row_even = iota((2 * modes, 1), 0) % 2 == 0

    @pl.when(is_owner)
    def _():
        whole(mode_recv, owners - 1, mode_sems(0)).wait_recv()

    @pl.when(jnp.logical_not(is_owner))
    def _():
        whole(mode_recv, owners, mode_sems(0)).wait_recv()

    columns = mm(expand, mode_recv[...].reshape(modes, width))
    masked = jnp.where(u_match, columns, 0.0)
    mean = jnp.sum(masked, axis=1, keepdims=True) * (1.0 / snap)
    centered = jnp.where(u_match, masked - mean, 0.0)
    moved = jnp.where(row_even, pltpu.roll(centered, 1, 1), pltpu.roll(centered, width - 1, 1))
    twice_ref[...] = (centered + moved).astype(BF)

    whole(send, lat_count - 1, block_sems).wait_send()

    @pl.when(is_owner)
    def _():
        whole(tail_send, owners - 1, tail_sems(field)).wait_send()
        whole(col_recv, lat_count, mode_sems(0)).wait_send()
        whole(col_recv, lat_count - 1, mode_sems(1)).wait_send()

    @pl.when(jnp.logical_not(is_owner))
    def _():
        whole(tail_send, owners, tail_sems(field)).wait_send()

    @pl.when((field == 1) & in_owners)
    def _():
        whole(col_send, owners - 1, col_sems).wait_send()

    @pl.when((field == 1) & jnp.logical_not(in_owners))
    def _():
        whole(col_send, owners, col_sems).wait_send()


def dft_constant(nord, lon):
    angles = (np.outer(np.arange(nord), np.arange(lon)) % lon) * (2.0 * math.pi / lon)
    return np.concatenate([np.cos(angles), -np.sin(angles)], axis=0).astype(np.float32).astype(BF)


def fused(lat_count, first, owners, fields_grid, basis, order_table, panel_modes):
    _, snap, _, pairs, lon = fields_grid.shape
    slots, pair_total, degs = basis.shape
    modes = panel_modes.shape[1]
    per = modes // owners
    width = 2 * snap
    block = 2 * slots
    head = pairs * block
    x = fields_grid[0].transpose(0, 2, 1, 3)
    table = jnp.asarray(dft_constant(degs, lon))
    vmem = pl.BlockSpec(memory_space=pltpu.VMEM)
    body = functools.partial(kernel, lat_count, snap, pairs, lon, slots, degs, first, owners, per)
    coef, twice = pl.pallas_call(
        body,
        out_shape=(
            jax.ShapeDtypeStruct((slots, 2 * degs, width), BF),
            jax.ShapeDtypeStruct((2 * modes, width), BF),
        ),
        in_specs=[pl.BlockSpec(memory_space=pl.ANY)] * 5,
        out_specs=(vmem, vmem),
        scratch_shapes=[
            pltpu.VMEM(x.shape, BF),
            pltpu.VMEM(basis.shape, BF),
            pltpu.VMEM(table.shape, BF),
            pltpu.VMEM((slots, lat_count), jnp.int32),
            pltpu.VMEM(panel_modes.shape, jnp.int32),
            pltpu.SemaphoreType.DMA((5,)),
            pltpu.VMEM((lat_count, head, width), BF),
            pltpu.VMEM((lat_count, head, width), BF),
            pltpu.VMEM((owners, pairs * per, width), BF),
            pltpu.VMEM((2, lat_count, pairs * per, width), BF),
            pltpu.VMEM((owners, per, width), BF),
            pltpu.VMEM((lat_count, per, width), BF),
            pltpu.VMEM((2, per, width), BF),
            pltpu.VMEM((owners, per, width), BF),
            pltpu.VMEM((lat_count * head, width), F32),
            pltpu.VMEM((slots, 2 * degs, 2 * pair_total), BF),
        ] + [pltpu.SemaphoreType.DMA] * 3 + [
            pltpu.SemaphoreType.DMA((2,)),
            pltpu.SemaphoreType.DMA,
            pltpu.SemaphoreType.DMA,
            pltpu.SemaphoreType.DMA((2,)),
            pltpu.SemaphoreType.DMA,
            pltpu.SemaphoreType.REGULAR,
        ],
        compiler_params=pltpu.CompilerParams(
            collective_id=0, has_side_effects=True, vmem_limit_bytes=52 * 1024 * 1024
        ),
    )(*[pltpu.with_memory_space_constraint(v, pltpu.HBM) for v in (x, basis, table, order_table.T, panel_modes)])
    panel = lax.dot_general(
        coef.reshape(slots * 2 * degs, width), twice, NT, preferred_element_type=F32
    ) * (1.0 / (snap - 1))
    return panel.astype(BF).reshape(1, slots, 2 * degs, 2 * modes)


def dft_table(orders, lon_count):
    valid_slot = orders >= 0
    safe_orders = jnp.maximum(orders, 0)
    products = lax.broadcasted_iota(jnp.int32, (lon_count, 1), 0) * safe_orders[None, :] % lon_count
    angles = products.astype(jnp.float32) * (2.0 * math.pi / lon_count)
    cosine = jnp.where(valid_slot[None, :], jnp.cos(angles), 0.0).astype(jnp.bfloat16)
    sine_table = jnp.where(valid_slot[None, :], -jnp.sin(angles), 0.0).astype(jnp.bfloat16)
    return jnp.stack([cosine, sine_table], axis=1)


def local(fields_grid, basis, order_table, panel_modes):
    grid_one = fields_grid[0]
    snap_count = grid_one.shape[0]
    pair_count = grid_one.shape[2]
    lon_count = grid_one.shape[3]
    slot_count = order_table.shape[1]
    deg_count = basis.shape[2]
    pair_total = basis.shape[1]
    mode_count = panel_modes.shape[1]
    orders = order_table.reshape(-1)
    slot_all = orders.shape[0]
    dft = dft_table(orders, lon_count)
    fourier = jnp.einsum("thjn,nrk->hkjrt", grid_one, dft, preferred_element_type=jnp.float32) * (
        1.0 / math.sqrt(lon_count)
    )
    fourier = fourier.reshape(2, slot_all, pair_count, 2 * snap_count)
    parity_parts = jnp.stack([fourier[0] + fourier[1], fourier[0] - fourier[1]]).astype(
        jnp.bfloat16
    )
    group_index = lax.axis_index("lat")
    my_orders = lax.dynamic_slice_in_dim(order_table, group_index, 1, 0)[0]
    my_odd = my_orders % 2 == 1
    basis_split = basis.reshape(slot_count, pair_total, deg_count // 2, 2)
    even_rows = basis_split[:, :, :, 0]
    odd_rows = basis_split[:, :, :, 1]
    degree = lax.broadcasted_iota(jnp.int32, (1, deg_count), 1)
    keep_mask = (degree >= my_orders[:, None]) & (my_orders >= 0)[:, None]
    received = lax.all_to_all(parity_parts, "lat", split_axis=1, concat_axis=2, tiled=True)
    first_parity = jnp.where(my_odd[:, None, None], received[1], received[0])
    second = jnp.where(my_odd[:, None, None], received[0], received[1])
    low_degrees = jnp.einsum(
        "sjh,sjc->shc", even_rows, first_parity, preferred_element_type=jnp.float32
    )
    high_degrees = jnp.einsum("sjh,sjc->shc", odd_rows, second, preferred_element_type=jnp.float32)
    joined = jnp.stack([low_degrees, high_degrees], axis=2).reshape(slot_count, deg_count, -1)
    coefficients = jnp.where(keep_mask[:, :, None], joined, 0.0).astype(jnp.bfloat16)
    mode_order = panel_modes[0]
    mode_degree = panel_modes[1]
    onehot = (my_orders[None, :] == mode_order[:, None]).astype(jnp.bfloat16)
    picked = jnp.take(coefficients, mode_degree, axis=1)
    local_values = jnp.einsum("ms,smc->mc", onehot, picked, preferred_element_type=jnp.float32)
    field_index = lax.axis_index("field")
    both_fields = jnp.stack(
        [
            jnp.where(field_index == 0, local_values, 0.0),
            jnp.where(field_index == 1, local_values, 0.0),
        ]
    )
    summed = lax.psum(both_fields, ("lat", "field"))
    other_field = jnp.where(field_index == 0, summed[1], summed[0]).astype(jnp.bfloat16)
    columns = other_field.astype(jnp.float32).reshape(mode_count * 2, snap_count)
    centered = (columns - jnp.mean(columns, axis=1, keepdims=True)).astype(jnp.bfloat16)
    coef_rows = coefficients.reshape(slot_count * deg_count * 2, snap_count)
    panel_values = lax.dot_general(
        coef_rows, centered, (((1,), (1,)), ((), ())), preferred_element_type=jnp.float32
    )
    panel_values = panel_values * (1.0 / (snap_count - 1))
    return panel_values.astype(jnp.bfloat16).reshape(1, slot_count, 2 * deg_count, 2 * mode_count)


def device_program(lat_count, fields_grid, basis, order_table, panel_modes):
    pairs, snap = fields_grid.shape[3], fields_grid.shape[1]
    slots, pair_total, degs = basis.shape
    modes = panel_modes.shape[1]
    first, owners = 3, lat_count // 2
    fits = (
        lat_count % 2 == 0
        and owners > first
        and modes % owners == 0
        and modes // owners == 8
        and 2 * snap == 128
        and slots == 8
        and degs <= 256
        and pair_total <= 2 * snap
        and lat_count * pairs * slots <= 512
    )
    if fits:
        return fused(lat_count, first, owners, fields_grid, basis, order_table, panel_modes)
    return local(fields_grid, basis, order_table, panel_modes)


def solution(mesh):
    placed = (P("field", None, None, "lat", None), P("lat", None, None), P(), P())
    return jax.shard_map(
        functools.partial(device_program, mesh.shape["lat"]),
        mesh=mesh, in_specs=placed, out_specs=P("field", "lat", None, None), check_vma=False,
    )
```

```python
import functools
import math

import jax
import jax.numpy as jnp
import numpy as np
from jax import lax
from jax.experimental import pallas as pl
from jax.experimental.pallas import tpu as pltpu
from jax.sharding import PartitionSpec as P

BF = jnp.bfloat16
F32 = jnp.float32
NT = (((1,), (1,)), ((), ()))


def iota(shape, dim):
    return lax.broadcasted_iota(jnp.int32, shape, dim)


def mm(a, b):
    return jnp.dot(a, b, preferred_element_type=F32)


def mm_nt(a, b):
    return lax.dot_general(a, b, NT, preferred_element_type=F32)


def kernel(
    lat_count, snap, pairs, lon, slots, degs, first, owners, per,
    x_hbm, basis_hbm, table_hbm, orders_hbm, modes_hbm,
    coef_ref, twice_ref,
    x_ref, basis_ref, table_ref, orders_ref, modes_ref, load_sem,
    send, recv, tail_send, tail_recv, col_send, col_recv, mode_send, mode_recv, wide, rows,
    send_sem, recv_sem, tail_send_sem, tail_recv_sem, col_send_sem, col_recv_sem,
    mode_send_sem, mode_recv_sem, late, ready,
):
    me = lax.axis_index("lat")
    field = lax.axis_index("field")
    other = 1 - field
    pair_total = lat_count * pairs
    width = 2 * snap
    block = 2 * slots
    slot_all = lat_count * slots
    modes = owners * per
    early = first + owners
    plane = lat_count // 4
    inner = me // plane * plane
    is_early = me < early
    in_owners = (me >= first) & (me < early)
    is_owner = in_owners & (field == 1)

    loads = [
        pltpu.make_async_copy(src, dst, load_sem.at[at])
        for at, (src, dst) in enumerate([
            (table_hbm, table_ref), (modes_hbm, modes_ref), (orders_hbm, orders_ref),
            (basis_hbm, basis_ref), (x_hbm, x_ref),
        ])
    ]
    for load in loads:
        load.start()

    barrier = pltpu.get_barrier_semaphore()

    def signal(sem, lat, core):
        pl.semaphore_signal(sem, inc=1, device_id=(lat, core), device_id_type=pl.DeviceIdType.MESH)

    def owns(lat):
        return (lat >= first) & (lat < early)

    def greet(lat, c):
        @pl.when((lat != me) & is_early)
        def _():
            signal(barrier, lat, field)

        @pl.when(is_early & (is_owner | ((field == 0) & owns(lat))))
        def _():
            signal(barrier, lat, other)
        return c

    lax.fori_loop(0, lat_count, greet, 0)

    nord = table_ref.shape[0] // 2
    loads[1].wait()
    loads[2].wait()
    diagonal = iota((modes, modes), 0) == iota((modes, modes), 1)
    mode_col = jnp.sum(jnp.where(diagonal, modes_ref[0:1, :], 0), axis=1, keepdims=True)
    deg_col = jnp.sum(jnp.where(diagonal, modes_ref[1:2, :], 0), axis=1, keepdims=True)
    mode_odd = ((deg_col - mode_col) & 1) == 1
    by_slot = orders_ref[...]
    my_orders = jnp.sum(
        jnp.where(iota((slots, lat_count), 1) == me, by_slot, 0), axis=1, keepdims=True
    )

    def waves(cosine_row, sine_row):
        want = jnp.concatenate([cosine_row, sine_row], axis=0)
        onehot = (iota((want.shape[0], 2 * nord), 1) == want).astype(F32).astype(BF)
        return mm(onehot, table_ref[...]).astype(BF)

    loads[0].wait()
    mode_dft = waves(mode_col, mode_col + nord)
    even_lane = iota((1, width), 1) % 2 == 0

    def hemispheres(table, j):
        wave = mm_nt(table, x_ref[:, j].reshape(width, lon)) * (1.0 / math.sqrt(lon))
        half = wave.shape[0] // 2
        real, imag = wave[:half], wave[half:]
        north = jnp.where(even_lane, real, pltpu.roll(imag, 1, 1))
        south = jnp.where(even_lane, pltpu.roll(real, width - 1, 1), imag)
        return north, south

    loads[4].wait()
    for j in range(pairs):
        north, south = hemispheres(mode_dft, j)
        part = jnp.where(mode_odd, north - south, north + south)
        tail_send[:, j * per:(j + 1) * per, :] = part.reshape(owners, per, width).astype(BF)

    across = jnp.where(field == 0, owners, jnp.where(is_owner, early, 0))
    across_late = jnp.where(field == 0, owners, 0)
    pl.semaphore_wait(
        barrier, jnp.where(is_early, early - 1 + across, early + across_late)
    )

    def remote(src, dst, sems, lat, core):
        return pltpu.make_async_remote_copy(
            src_ref=src, dst_ref=dst, send_sem=sems[0], recv_sem=sems[1],
            device_id=(lat, core), device_id_type=pl.DeviceIdType.MESH,
        )

    block_sems = (send_sem, recv_sem)
    col_sems = (col_send_sem, col_recv_sem)

    def mode_sems(core):
        return (mode_send_sem.at[core], mode_recv_sem)

    def tail_sems(core):
        return (tail_send_sem, tail_recv_sem.at[core])

    def whole(ref, count, sems):
        part = ref.at[pl.ds(0, count)]
        return remote(part, part, sems, me, other)

    def start_tail(at, c):
        @pl.when((field == 0) | (at + first != me))
        def _():
            remote(tail_send.at[at], tail_recv.at[field, me], tail_sems(field), at + first, 1).start()
        return c

    lax.fori_loop(0, owners, start_tail, 0)
    loads[3].wait()

    @pl.when(field == 1)
    def _():
        cols = jnp.zeros((modes, pair_total), F32)
        at_degree = iota((modes, degs), 1) == deg_col
        for s in range(slots):
            pick = at_degree & (mode_col == my_orders[s:s + 1, :])
            cols = cols + mm_nt(pick.astype(F32).astype(BF), basis_ref[s])
        cols = jnp.concatenate([cols, jnp.zeros((modes, width - pair_total), F32)], axis=1)
        col_send[...] = cols.reshape(owners, per, width).astype(BF)

        def start_col(at, c):
            @pl.when(at + first != me)
            def _():
                remote(col_send.at[at], col_recv.at[me], col_sems, at + first, 1).start()
            return c

        lax.fori_loop(0, owners, start_col, 0)

    @pl.when(jnp.logical_not(is_early))
    def _():
        def arrive(lat, c):
            signal(late, lat, field)

            @pl.when((field == 0) & owns(lat))
            def _():
                signal(late, lat, other)
            return c

        lax.fori_loop(0, early, arrive, 0)

    tiled = jnp.concatenate([by_slot] * lat_count, axis=0)
    here = iota((slot_all, lat_count), 1) == iota((slot_all, lat_count), 0) // slots
    order_col = jnp.sum(jnp.where(here, tiled, 0), axis=1, keepdims=True)
    slot_dft = waves(order_col, jnp.where(order_col >= 0, order_col + nord, -1))
    for j in range(pairs):
        north, south = hemispheres(slot_dft, j)
        shape = (lat_count, slots, width)
        both = jnp.concatenate([(north + south).reshape(shape), (north - south).reshape(shape)], axis=1)
        send[:, j * block:(j + 1) * block, :] = both.astype(BF)

    def start_block(lat, c):
        @pl.when(lat != me)
        def _():
            remote(send.at[lat], recv.at[me], block_sems, lat, field).start()
        return c

    lax.fori_loop(0, 1, start_block, 0)

    dup = (iota((2 * degs, degs), 0) // 2 == iota((2 * degs, degs), 1)).astype(F32).astype(BF)
    twin = (iota((pair_total, 2 * pair_total), 1) // 2 == iota((pair_total, 2 * pair_total), 0))
    twin = twin.astype(F32).astype(BF)
    deg = iota((2 * degs, 2 * pair_total), 0) // 2
    parity = iota((2 * degs, 2 * pair_total), 1) & 1
    for s in range(slots):
        order = my_orders[s:s + 1, :]
        base = mm(mm_nt(dup, basis_ref[s]).astype(BF), twin)
        keep = (deg >= order) & (order >= 0) & (((deg - order) & 1) == parity)
        rows[s] = jnp.where(keep, base, 0.0).astype(BF)

    lax.fori_loop(jnp.maximum(inner, 1), early, start_block, 0)

    @pl.when(me < lat_count // 2)
    def _():
        lax.fori_loop(1, jnp.minimum(inner, early), start_block, 0)

    @pl.when(is_early)
    def _():
        pl.semaphore_wait(late, (lat_count - early) * jnp.where(is_owner, 2, 1))

        @pl.when(me == early - 1)
        def _():
            def tell(lat, c):
                signal(ready, lat, field)
                return c

            lax.fori_loop(early, lat_count, tell, 0)

        lax.fori_loop(early, lat_count, start_block, 0)

    @pl.when(jnp.logical_not(is_owner) & (me >= lat_count // 2))
    def _():
        lax.fori_loop(1, jnp.minimum(inner, early), start_block, 0)

    @pl.when(jnp.logical_not(is_early))
    def _():
        pl.semaphore_wait(ready, 1)
        lax.fori_loop(early, lat_count, start_block, 0)

    recv[me] = send[me]

    @pl.when(is_owner)
    def _():
        tail_recv[1, me] = tail_send[me - first]
        col_recv[me] = col_send[me - first]
        total = lat_count * pairs * per
        place = iota((width, total), 1)
        spread = iota((width, total), 0) == place // (pairs * per) * pairs + place // per % pairs
        own = iota((per, total), 0) == iota((per, total), 1) % per
        whole(col_recv, lat_count - 1, col_sems).wait_recv()
        column = jnp.sum(col_recv[...].astype(F32), axis=0).astype(BF)
        weights = jnp.where(own, mm(column, spread.astype(F32).astype(BF)), 0.0).astype(BF)

        def value_of(core):
            return mm(weights, tail_recv[core].reshape(total, width)).astype(BF)

        def start_mode(core):
            def start(lat, c):
                @pl.when((core == 0) | (lat != me))
                def _():
                    remote(
                        mode_send.at[1 - core], mode_recv.at[me - first], mode_sems(core), lat, core
                    ).start()
                return c

            lax.fori_loop(0, lat_count, start, 0)

        whole(tail_recv.at[1], lat_count - 1, tail_sems(1)).wait_recv()
        mode_send[1] = value_of(1)
        start_mode(0)
        whole(tail_recv.at[0], lat_count, tail_sems(0)).wait_recv()
        mode_send[0] = value_of(0)
        start_mode(1)

        @pl.when(me >= lat_count // 2)
        def _():
            lax.fori_loop(1, jnp.minimum(inner, early), start_block, 0)

        mode_recv[me - first] = mode_send[0]

    expand = (iota((2 * modes, modes), 1) == iota((2 * modes, modes), 0) // 2).astype(F32).astype(BF)
    u_match = iota((2 * modes, width), 1) % 2 == iota((2 * modes, width), 0) % 2
    row_even = iota((2 * modes, 1), 0) % 2 == 0
    same_r = iota((2 * degs, width), 1) % 2 == iota((2 * degs, width), 0) % 2

    def take_blocks():
        whole(recv, lat_count - 1, block_sems).wait_recv()
        wide[...] = recv[...].reshape(slot_all * 2 * pairs, width).astype(F32)
        for s in range(slots):
            picked = wide[pl.ds(s, 2 * pair_total, stride=slots), :].astype(BF)
            coef_ref[s] = jnp.where(same_r, mm(rows[s], picked), 0.0).astype(BF)

    def take_modes():
        @pl.when(is_owner)
        def _():
            whole(mode_recv, owners - 1, mode_sems(0)).wait_recv()

        @pl.when(jnp.logical_not(is_owner))
        def _():
            whole(mode_recv, owners, mode_sems(0)).wait_recv()

        columns = mm(expand, mode_recv[...].reshape(modes, width))
        masked = jnp.where(u_match, columns, 0.0)
        mean = jnp.sum(masked, axis=1, keepdims=True) * (1.0 / snap)
        centered = jnp.where(u_match, masked - mean, 0.0)
        moved = jnp.where(row_even, pltpu.roll(centered, 1, 1), pltpu.roll(centered, width - 1, 1))
        twice_ref[...] = (centered + moved).astype(BF)

    modes_first = (me > 0) & (me < lat_count // 2)

    @pl.when(modes_first)
    def _():
        take_modes()
        take_blocks()

    @pl.when(jnp.logical_not(modes_first))
    def _():
        take_blocks()
        take_modes()

    whole(send, lat_count - 1, block_sems).wait_send()

    @pl.when(is_owner)
    def _():
        whole(tail_send, owners - 1, tail_sems(field)).wait_send()
        whole(col_recv, lat_count, mode_sems(0)).wait_send()
        whole(col_recv, lat_count - 1, mode_sems(1)).wait_send()

    @pl.when(jnp.logical_not(is_owner))
    def _():
        whole(tail_send, owners, tail_sems(field)).wait_send()

    @pl.when((field == 1) & in_owners)
    def _():
        whole(col_send, owners - 1, col_sems).wait_send()

    @pl.when((field == 1) & jnp.logical_not(in_owners))
    def _():
        whole(col_send, owners, col_sems).wait_send()


def dft_constant(nord, lon):
    angles = (np.outer(np.arange(nord), np.arange(lon)) % lon) * (2.0 * math.pi / lon)
    return np.concatenate([np.cos(angles), -np.sin(angles)], axis=0).astype(np.float32).astype(BF)


def fused(lat_count, first, owners, fields_grid, basis, order_table, panel_modes):
    _, snap, _, pairs, lon = fields_grid.shape
    slots, pair_total, degs = basis.shape
    modes = panel_modes.shape[1]
    per = modes // owners
    width = 2 * snap
    block = 2 * slots
    head = pairs * block
    x = fields_grid[0].transpose(0, 2, 1, 3)
    table = jnp.asarray(dft_constant(degs, lon))
    vmem = pl.BlockSpec(memory_space=pltpu.VMEM)
    body = functools.partial(kernel, lat_count, snap, pairs, lon, slots, degs, first, owners, per)
    coef, twice = pl.pallas_call(
        body,
        out_shape=(
            jax.ShapeDtypeStruct((slots, 2 * degs, width), BF),
            jax.ShapeDtypeStruct((2 * modes, width), BF),
        ),
        in_specs=[pl.BlockSpec(memory_space=pl.ANY)] * 5,
        out_specs=(vmem, vmem),
        scratch_shapes=[
            pltpu.VMEM(x.shape, BF),
            pltpu.VMEM(basis.shape, BF),
            pltpu.VMEM(table.shape, BF),
            pltpu.VMEM((slots, lat_count), jnp.int32),
            pltpu.VMEM(panel_modes.shape, jnp.int32),
            pltpu.SemaphoreType.DMA((5,)),
            pltpu.VMEM((lat_count, head, width), BF),
            pltpu.VMEM((lat_count, head, width), BF),
            pltpu.VMEM((owners, pairs * per, width), BF),
            pltpu.VMEM((2, lat_count, pairs * per, width), BF),
            pltpu.VMEM((owners, per, width), BF),
            pltpu.VMEM((lat_count, per, width), BF),
            pltpu.VMEM((2, per, width), BF),
            pltpu.VMEM((owners, per, width), BF),
            pltpu.VMEM((lat_count * head, width), F32),
            pltpu.VMEM((slots, 2 * degs, 2 * pair_total), BF),
        ] + [pltpu.SemaphoreType.DMA] * 3 + [
            pltpu.SemaphoreType.DMA((2,)),
            pltpu.SemaphoreType.DMA,
            pltpu.SemaphoreType.DMA,
            pltpu.SemaphoreType.DMA((2,)),
            pltpu.SemaphoreType.DMA,
            pltpu.SemaphoreType.REGULAR,
            pltpu.SemaphoreType.REGULAR,
        ],
        compiler_params=pltpu.CompilerParams(
            collective_id=0, has_side_effects=True, vmem_limit_bytes=52 * 1024 * 1024
        ),
    )(*[pltpu.with_memory_space_constraint(v, pltpu.HBM) for v in (x, basis, table, order_table.T, panel_modes)])
    panel = lax.dot_general(
        coef.reshape(slots * 2 * degs, width), twice, NT, preferred_element_type=F32
    ) * (1.0 / (snap - 1))
    return panel.astype(BF).reshape(1, slots, 2 * degs, 2 * modes)


def dft_table(orders, lon_count):
    valid_slot = orders >= 0
    safe_orders = jnp.maximum(orders, 0)
    products = lax.broadcasted_iota(jnp.int32, (lon_count, 1), 0) * safe_orders[None, :] % lon_count
    angles = products.astype(jnp.float32) * (2.0 * math.pi / lon_count)
    cosine = jnp.where(valid_slot[None, :], jnp.cos(angles), 0.0).astype(jnp.bfloat16)
    sine_table = jnp.where(valid_slot[None, :], -jnp.sin(angles), 0.0).astype(jnp.bfloat16)
    return jnp.stack([cosine, sine_table], axis=1)


def local(fields_grid, basis, order_table, panel_modes):
    grid_one = fields_grid[0]
    snap_count = grid_one.shape[0]
    pair_count = grid_one.shape[2]
    lon_count = grid_one.shape[3]
    slot_count = order_table.shape[1]
    deg_count = basis.shape[2]
    pair_total = basis.shape[1]
    mode_count = panel_modes.shape[1]
    orders = order_table.reshape(-1)
    slot_all = orders.shape[0]
    dft = dft_table(orders, lon_count)
    fourier = jnp.einsum("thjn,nrk->hkjrt", grid_one, dft, preferred_element_type=jnp.float32) * (
        1.0 / math.sqrt(lon_count)
    )
    fourier = fourier.reshape(2, slot_all, pair_count, 2 * snap_count)
    parity_parts = jnp.stack([fourier[0] + fourier[1], fourier[0] - fourier[1]]).astype(
        jnp.bfloat16
    )
    group_index = lax.axis_index("lat")
    my_orders = lax.dynamic_slice_in_dim(order_table, group_index, 1, 0)[0]
    my_odd = my_orders % 2 == 1
    basis_split = basis.reshape(slot_count, pair_total, deg_count // 2, 2)
    even_rows = basis_split[:, :, :, 0]
    odd_rows = basis_split[:, :, :, 1]
    degree = lax.broadcasted_iota(jnp.int32, (1, deg_count), 1)
    keep_mask = (degree >= my_orders[:, None]) & (my_orders >= 0)[:, None]
    received = lax.all_to_all(parity_parts, "lat", split_axis=1, concat_axis=2, tiled=True)
    first_parity = jnp.where(my_odd[:, None, None], received[1], received[0])
    second = jnp.where(my_odd[:, None, None], received[0], received[1])
    low_degrees = jnp.einsum(
        "sjh,sjc->shc", even_rows, first_parity, preferred_element_type=jnp.float32
    )
    high_degrees = jnp.einsum("sjh,sjc->shc", odd_rows, second, preferred_element_type=jnp.float32)
    joined = jnp.stack([low_degrees, high_degrees], axis=2).reshape(slot_count, deg_count, -1)
    coefficients = jnp.where(keep_mask[:, :, None], joined, 0.0).astype(jnp.bfloat16)
    mode_order = panel_modes[0]
    mode_degree = panel_modes[1]
    onehot = (my_orders[None, :] == mode_order[:, None]).astype(jnp.bfloat16)
    picked = jnp.take(coefficients, mode_degree, axis=1)
    local_values = jnp.einsum("ms,smc->mc", onehot, picked, preferred_element_type=jnp.float32)
    field_index = lax.axis_index("field")
    both_fields = jnp.stack(
        [
            jnp.where(field_index == 0, local_values, 0.0),
            jnp.where(field_index == 1, local_values, 0.0),
        ]
    )
    summed = lax.psum(both_fields, ("lat", "field"))
    other_field = jnp.where(field_index == 0, summed[1], summed[0]).astype(jnp.bfloat16)
    columns = other_field.astype(jnp.float32).reshape(mode_count * 2, snap_count)
    centered = (columns - jnp.mean(columns, axis=1, keepdims=True)).astype(jnp.bfloat16)
    coef_rows = coefficients.reshape(slot_count * deg_count * 2, snap_count)
    panel_values = lax.dot_general(
        coef_rows, centered, (((1,), (1,)), ((), ())), preferred_element_type=jnp.float32
    )
    panel_values = panel_values * (1.0 / (snap_count - 1))
    return panel_values.astype(jnp.bfloat16).reshape(1, slot_count, 2 * deg_count, 2 * mode_count)


def device_program(lat_count, fields_grid, basis, order_table, panel_modes):
    pairs, snap = fields_grid.shape[3], fields_grid.shape[1]
    slots, pair_total, degs = basis.shape
    modes = panel_modes.shape[1]
    first, owners = 3, lat_count // 2
    fits = (
        lat_count % 2 == 0
        and owners > first
        and modes % owners == 0
        and modes // owners == 8
        and 2 * snap == 128
        and slots == 8
        and degs <= 256
        and pair_total <= 2 * snap
        and lat_count * pairs * slots <= 512
    )
    if fits:
        return fused(lat_count, first, owners, fields_grid, basis, order_table, panel_modes)
    return local(fields_grid, basis, order_table, panel_modes)


def solution(mesh):
    placed = (P("field", None, None, "lat", None), P("lat", None, None), P(), P())
    return jax.shard_map(
        functools.partial(device_program, mesh.shape["lat"]),
        mesh=mesh, in_specs=placed, out_specs=P("field", "lat", None, None), check_vma=False,
    )
```

```python
import functools
import math

import jax
import jax.numpy as jnp
import numpy as np
from jax import lax
from jax.experimental import pallas as pl
from jax.experimental.pallas import tpu as pltpu
from jax.sharding import PartitionSpec as P

BF = jnp.bfloat16
F32 = jnp.float32
NT = (((1,), (1,)), ((), ()))


def iota(shape, dim):
    return lax.broadcasted_iota(jnp.int32, shape, dim)


def mm(a, b):
    return jnp.dot(a, b, preferred_element_type=F32)


def mm_nt(a, b):
    return lax.dot_general(a, b, NT, preferred_element_type=F32)


def kernel(
    lat_count, snap, pairs, lon, slots, degs, first, owners, per,
    x_hbm, basis_hbm, table_hbm, orders_hbm, modes_hbm,
    coef_ref, twice_ref,
    x_ref, basis_ref, table_ref, orders_ref, modes_ref, load_sem,
    send, recv, tail_send, tail_recv, col_send, col_recv, mode_send, mode_recv, wide, rows,
    send_sem, recv_sem, tail_send_sem, tail_recv_sem, col_send_sem, col_recv_sem,
    mode_send_sem, mode_recv_sem, late, ready,
):
    me = lax.axis_index("lat")
    field = lax.axis_index("field")
    other = 1 - field
    pair_total = lat_count * pairs
    width = 2 * snap
    block = 2 * slots
    slot_all = lat_count * slots
    modes = owners * per
    early = first + owners
    plane = lat_count // 4
    inner = me // plane * plane
    outer = lat_count - plane
    is_early = me < early
    in_owners = (me >= first) & (me < early)
    is_owner = in_owners & (field == 1)

    loads = [
        pltpu.make_async_copy(src, dst, load_sem.at[at])
        for at, (src, dst) in enumerate([
            (table_hbm, table_ref), (modes_hbm, modes_ref), (orders_hbm, orders_ref),
            (basis_hbm, basis_ref), (x_hbm, x_ref),
        ])
    ]
    for load in loads:
        load.start()

    barrier = pltpu.get_barrier_semaphore()

    def signal(sem, lat, core):
        pl.semaphore_signal(sem, inc=1, device_id=(lat, core), device_id_type=pl.DeviceIdType.MESH)

    def owns(lat):
        return (lat >= first) & (lat < early)

    def greet(at, c):
        lat = lat_count - 1 - at

        @pl.when((lat != me) & is_early)
        def _():
            signal(barrier, lat, field)

        @pl.when(is_early & (is_owner | ((field == 0) & owns(lat))))
        def _():
            signal(barrier, lat, other)
        return c

    lax.fori_loop(0, lat_count, greet, 0, unroll=True)

    nord = table_ref.shape[0] // 2
    loads[1].wait()
    loads[2].wait()
    diagonal = iota((modes, modes), 0) == iota((modes, modes), 1)
    mode_col = jnp.sum(jnp.where(diagonal, modes_ref[0:1, :], 0), axis=1, keepdims=True)
    deg_col = jnp.sum(jnp.where(diagonal, modes_ref[1:2, :], 0), axis=1, keepdims=True)
    mode_odd = ((deg_col - mode_col) & 1) == 1
    by_slot = orders_ref[...]
    my_orders = jnp.sum(
        jnp.where(iota((slots, lat_count), 1) == me, by_slot, 0), axis=1, keepdims=True
    )

    def waves(cosine_row, sine_row):
        want = jnp.concatenate([cosine_row, sine_row], axis=0)
        onehot = (iota((want.shape[0], 2 * nord), 1) == want).astype(F32).astype(BF)
        return mm(onehot, table_ref[...]).astype(BF)

    loads[0].wait()
    mode_dft = waves(mode_col, mode_col + nord)
    even_lane = iota((1, width), 1) % 2 == 0

    def hemispheres(table, j):
        wave = mm_nt(table, x_ref[:, j].reshape(width, lon)) * (1.0 / math.sqrt(lon))
        half = wave.shape[0] // 2
        real, imag = wave[:half], wave[half:]
        north = jnp.where(even_lane, real, pltpu.roll(imag, 1, 1))
        south = jnp.where(even_lane, pltpu.roll(real, width - 1, 1), imag)
        return north, south

    loads[4].wait()
    for j in range(pairs):
        north, south = hemispheres(mode_dft, j)
        part = jnp.where(mode_odd, north - south, north + south)
        tail_send[:, j * per:(j + 1) * per, :] = part.reshape(owners, per, width).astype(BF)

    across = jnp.where(field == 0, owners, jnp.where(is_owner, early, 0))
    across_late = jnp.where(field == 0, owners, 0)
    pl.semaphore_wait(
        barrier, jnp.where(is_early, early - 1 + across, early + across_late)
    )

    def remote(src, dst, sems, lat, core):
        return pltpu.make_async_remote_copy(
            src_ref=src, dst_ref=dst, send_sem=sems[0], recv_sem=sems[1],
            device_id=(lat, core), device_id_type=pl.DeviceIdType.MESH,
        )

    block_sems = (send_sem, recv_sem)
    col_sems = (col_send_sem, col_recv_sem)

    def mode_sems(core):
        return (mode_send_sem.at[core], mode_recv_sem)

    def tail_sems(core):
        return (tail_send_sem, tail_recv_sem.at[core])

    def whole(ref, count, sems):
        part = ref.at[pl.ds(0, count)]
        return remote(part, part, sems, me, other)

    def start_tail(at, c):
        @pl.when((field == 0) | (at + first != me))
        def _():
            remote(tail_send.at[at], tail_recv.at[field, me], tail_sems(field), at + first, 1).start()
        return c

    lax.fori_loop(0, owners, start_tail, 0)
    loads[3].wait()

    @pl.when(field == 1)
    def _():
        cols = jnp.zeros((modes, pair_total), F32)
        at_degree = iota((modes, degs), 1) == deg_col
        for s in range(slots):
            pick = at_degree & (mode_col == my_orders[s:s + 1, :])
            cols = cols + mm_nt(pick.astype(F32).astype(BF), basis_ref[s])
        cols = jnp.concatenate([cols, jnp.zeros((modes, width - pair_total), F32)], axis=1)
        col_send[...] = cols.reshape(owners, per, width).astype(BF)

        def start_col(at, c):
            @pl.when(at + first != me)
            def _():
                remote(col_send.at[at], col_recv.at[me], col_sems, at + first, 1).start()
            return c

        lax.fori_loop(0, owners, start_col, 0)

    @pl.when(jnp.logical_not(is_early))
    def _():
        def arrive(lat, c):
            signal(late, lat, field)

            @pl.when((field == 0) & owns(lat))
            def _():
                signal(late, lat, other)
            return c

        lax.fori_loop(0, early, arrive, 0)

    tiled = jnp.concatenate([by_slot] * lat_count, axis=0)
    here = iota((slot_all, lat_count), 1) == iota((slot_all, lat_count), 0) // slots
    order_col = jnp.sum(jnp.where(here, tiled, 0), axis=1, keepdims=True)
    slot_dft = waves(order_col, jnp.where(order_col >= 0, order_col + nord, -1))
    for j in range(pairs):
        north, south = hemispheres(slot_dft, j)
        shape = (lat_count, slots, width)
        both = jnp.concatenate([(north + south).reshape(shape), (north - south).reshape(shape)], axis=1)
        send[:, j * block:(j + 1) * block, :] = both.astype(BF)

    def start_block(lat, c):
        @pl.when(lat != me)
        def _():
            remote(send.at[lat], recv.at[me], block_sems, lat, field).start()
        return c

    lax.fori_loop(0, 1, start_block, 0)

    dup = (iota((2 * degs, degs), 0) // 2 == iota((2 * degs, degs), 1)).astype(F32).astype(BF)
    twin = (iota((pair_total, 2 * pair_total), 1) // 2 == iota((pair_total, 2 * pair_total), 0))
    twin = twin.astype(F32).astype(BF)
    deg = iota((2 * degs, 2 * pair_total), 0) // 2
    parity = iota((2 * degs, 2 * pair_total), 1) & 1
    for s in range(slots):
        order = my_orders[s:s + 1, :]
        base = mm(mm_nt(dup, basis_ref[s]).astype(BF), twin)
        keep = (deg >= order) & (order >= 0) & (((deg - order) & 1) == parity)
        rows[s] = jnp.where(keep, base, 0.0).astype(BF)

    lax.fori_loop(jnp.maximum(inner, 1), early, start_block, 0)

    @pl.when(me < lat_count // 2)
    def _():
        lax.fori_loop(1, jnp.minimum(inner, early), start_block, 0)

    @pl.when(is_early)
    def _():
        pl.semaphore_wait(late, (lat_count - early) * jnp.where(is_owner, 2, 1))

        @pl.when(me == early - 1)
        def _():
            def tell(lat, c):
                signal(ready, lat, field)
                return c

            lax.fori_loop(early, lat_count, tell, 0)

        lax.fori_loop(outer, jnp.where(is_owner, outer + 1, outer), start_block, 0)

        @pl.when(jnp.logical_not(is_owner))
        def _():
            lax.fori_loop(early, lat_count, start_block, 0)

    @pl.when(jnp.logical_not(is_owner) & (me >= lat_count // 2))
    def _():
        lax.fori_loop(1, jnp.minimum(inner, early), start_block, 0)

    @pl.when(jnp.logical_not(is_early))
    def _():
        pl.semaphore_wait(ready, 1)
        lax.fori_loop(early, lat_count, start_block, 0)

    recv[me] = send[me]

    @pl.when(is_owner)
    def _():
        tail_recv[1, me] = tail_send[me - first]
        col_recv[me] = col_send[me - first]
        total = lat_count * pairs * per
        place = iota((width, total), 1)
        spread = iota((width, total), 0) == place // (pairs * per) * pairs + place // per % pairs
        own = iota((per, total), 0) == iota((per, total), 1) % per
        whole(col_recv, lat_count - 1, col_sems).wait_recv()
        column = jnp.sum(col_recv[...].astype(F32), axis=0).astype(BF)
        weights = jnp.where(own, mm(column, spread.astype(F32).astype(BF)), 0.0).astype(BF)

        def value_of(core):
            return mm(weights, tail_recv[core].reshape(total, width)).astype(BF)

        def start_mode(core):
            def start(lat, c):
                @pl.when((core == 0) | (lat != me))
                def _():
                    remote(
                        mode_send.at[1 - core], mode_recv.at[me - first], mode_sems(core), lat, core
                    ).start()
                return c

            lax.fori_loop(0, lat_count, start, 0)

        whole(tail_recv.at[1], lat_count - 1, tail_sems(1)).wait_recv()
        mode_send[1] = value_of(1)
        start_mode(0)
        whole(tail_recv.at[0], lat_count, tail_sems(0)).wait_recv()
        mode_send[0] = value_of(0)
        start_mode(1)

        @pl.when(me >= lat_count // 2)
        def _():
            lax.fori_loop(1, jnp.minimum(inner, early), start_block, 0)

        lax.fori_loop(early, outer, start_block, 0)
        lax.fori_loop(outer + 1, lat_count, start_block, 0)
        mode_recv[me - first] = mode_send[0]

    expand = (iota((2 * modes, modes), 1) == iota((2 * modes, modes), 0) // 2).astype(F32).astype(BF)
    u_match = iota((2 * modes, width), 1) % 2 == iota((2 * modes, width), 0) % 2
    row_even = iota((2 * modes, 1), 0) % 2 == 0
    same_r = iota((2 * degs, width), 1) % 2 == iota((2 * degs, width), 0) % 2

    def take_blocks():
        whole(recv, lat_count - 1, block_sems).wait_recv()
        wide[...] = recv[...].reshape(slot_all * 2 * pairs, width).astype(F32)
        for s in range(slots):
            picked = wide[pl.ds(s, 2 * pair_total, stride=slots), :].astype(BF)
            coef_ref[s] = jnp.where(same_r, mm(rows[s], picked), 0.0).astype(BF)

    def take_modes():
        @pl.when(is_owner)
        def _():
            whole(mode_recv, owners - 1, mode_sems(0)).wait_recv()

        @pl.when(jnp.logical_not(is_owner))
        def _():
            whole(mode_recv, owners, mode_sems(0)).wait_recv()

        columns = mm(expand, mode_recv[...].reshape(modes, width))
        masked = jnp.where(u_match, columns, 0.0)
        mean = jnp.sum(masked, axis=1, keepdims=True) * (1.0 / snap)
        centered = jnp.where(u_match, masked - mean, 0.0)
        moved = jnp.where(row_even, pltpu.roll(centered, 1, 1), pltpu.roll(centered, width - 1, 1))
        twice_ref[...] = (centered + moved).astype(BF)

    modes_first = (me > 0) & (me < lat_count // 2)

    @pl.when(modes_first)
    def _():
        take_modes()
        take_blocks()

    @pl.when(jnp.logical_not(modes_first))
    def _():
        take_blocks()
        take_modes()

    whole(send, lat_count - 1, block_sems).wait_send()

    @pl.when(is_owner)
    def _():
        whole(tail_send, owners - 1, tail_sems(field)).wait_send()
        whole(col_recv, lat_count, mode_sems(0)).wait_send()
        whole(col_recv, lat_count - 1, mode_sems(1)).wait_send()

    @pl.when(jnp.logical_not(is_owner))
    def _():
        whole(tail_send, owners, tail_sems(field)).wait_send()

    @pl.when((field == 1) & in_owners)
    def _():
        whole(col_send, owners - 1, col_sems).wait_send()

    @pl.when((field == 1) & jnp.logical_not(in_owners))
    def _():
        whole(col_send, owners, col_sems).wait_send()


def dft_constant(nord, lon):
    angles = (np.outer(np.arange(nord), np.arange(lon)) % lon) * (2.0 * math.pi / lon)
    return np.concatenate([np.cos(angles), -np.sin(angles)], axis=0).astype(np.float32).astype(BF)


def fused(lat_count, first, owners, fields_grid, basis, order_table, panel_modes):
    _, snap, _, pairs, lon = fields_grid.shape
    slots, pair_total, degs = basis.shape
    modes = panel_modes.shape[1]
    per = modes // owners
    width = 2 * snap
    block = 2 * slots
    head = pairs * block
    x = fields_grid[0].transpose(0, 2, 1, 3)
    table = jnp.asarray(dft_constant(degs, lon))
    vmem = pl.BlockSpec(memory_space=pltpu.VMEM)
    body = functools.partial(kernel, lat_count, snap, pairs, lon, slots, degs, first, owners, per)
    coef, twice = pl.pallas_call(
        body,
        out_shape=(
            jax.ShapeDtypeStruct((slots, 2 * degs, width), BF),
            jax.ShapeDtypeStruct((2 * modes, width), BF),
        ),
        in_specs=[pl.BlockSpec(memory_space=pl.ANY)] * 5,
        out_specs=(vmem, vmem),
        scratch_shapes=[
            pltpu.VMEM(x.shape, BF),
            pltpu.VMEM(basis.shape, BF),
            pltpu.VMEM(table.shape, BF),
            pltpu.VMEM((slots, lat_count), jnp.int32),
            pltpu.VMEM(panel_modes.shape, jnp.int32),
            pltpu.SemaphoreType.DMA((5,)),
            pltpu.VMEM((lat_count, head, width), BF),
            pltpu.VMEM((lat_count, head, width), BF),
            pltpu.VMEM((owners, pairs * per, width), BF),
            pltpu.VMEM((2, lat_count, pairs * per, width), BF),
            pltpu.VMEM((owners, per, width), BF),
            pltpu.VMEM((lat_count, per, width), BF),
            pltpu.VMEM((2, per, width), BF),
            pltpu.VMEM((owners, per, width), BF),
            pltpu.VMEM((lat_count * head, width), F32),
            pltpu.VMEM((slots, 2 * degs, 2 * pair_total), BF),
        ] + [pltpu.SemaphoreType.DMA] * 3 + [
            pltpu.SemaphoreType.DMA((2,)),
            pltpu.SemaphoreType.DMA,
            pltpu.SemaphoreType.DMA,
            pltpu.SemaphoreType.DMA((2,)),
            pltpu.SemaphoreType.DMA,
            pltpu.SemaphoreType.REGULAR,
            pltpu.SemaphoreType.REGULAR,
        ],
        compiler_params=pltpu.CompilerParams(
            collective_id=0, has_side_effects=True, vmem_limit_bytes=52 * 1024 * 1024
        ),
    )(*[pltpu.with_memory_space_constraint(v, pltpu.HBM) for v in (x, basis, table, order_table.T, panel_modes)])
    panel = lax.dot_general(
        coef.reshape(slots * 2 * degs, width), twice, NT, preferred_element_type=F32
    ) * (1.0 / (snap - 1))
    return panel.astype(BF).reshape(1, slots, 2 * degs, 2 * modes)


def dft_table(orders, lon_count):
    valid_slot = orders >= 0
    safe_orders = jnp.maximum(orders, 0)
    products = lax.broadcasted_iota(jnp.int32, (lon_count, 1), 0) * safe_orders[None, :] % lon_count
    angles = products.astype(jnp.float32) * (2.0 * math.pi / lon_count)
    cosine = jnp.where(valid_slot[None, :], jnp.cos(angles), 0.0).astype(jnp.bfloat16)
    sine_table = jnp.where(valid_slot[None, :], -jnp.sin(angles), 0.0).astype(jnp.bfloat16)
    return jnp.stack([cosine, sine_table], axis=1)


def local(fields_grid, basis, order_table, panel_modes):
    grid_one = fields_grid[0]
    snap_count = grid_one.shape[0]
    pair_count = grid_one.shape[2]
    lon_count = grid_one.shape[3]
    slot_count = order_table.shape[1]
    deg_count = basis.shape[2]
    pair_total = basis.shape[1]
    mode_count = panel_modes.shape[1]
    orders = order_table.reshape(-1)
    slot_all = orders.shape[0]
    dft = dft_table(orders, lon_count)
    fourier = jnp.einsum("thjn,nrk->hkjrt", grid_one, dft, preferred_element_type=jnp.float32) * (
        1.0 / math.sqrt(lon_count)
    )
    fourier = fourier.reshape(2, slot_all, pair_count, 2 * snap_count)
    parity_parts = jnp.stack([fourier[0] + fourier[1], fourier[0] - fourier[1]]).astype(
        jnp.bfloat16
    )
    group_index = lax.axis_index("lat")
    my_orders = lax.dynamic_slice_in_dim(order_table, group_index, 1, 0)[0]
    my_odd = my_orders % 2 == 1
    basis_split = basis.reshape(slot_count, pair_total, deg_count // 2, 2)
    even_rows = basis_split[:, :, :, 0]
    odd_rows = basis_split[:, :, :, 1]
    degree = lax.broadcasted_iota(jnp.int32, (1, deg_count), 1)
    keep_mask = (degree >= my_orders[:, None]) & (my_orders >= 0)[:, None]
    received = lax.all_to_all(parity_parts, "lat", split_axis=1, concat_axis=2, tiled=True)
    first_parity = jnp.where(my_odd[:, None, None], received[1], received[0])
    second = jnp.where(my_odd[:, None, None], received[0], received[1])
    low_degrees = jnp.einsum(
        "sjh,sjc->shc", even_rows, first_parity, preferred_element_type=jnp.float32
    )
    high_degrees = jnp.einsum("sjh,sjc->shc", odd_rows, second, preferred_element_type=jnp.float32)
    joined = jnp.stack([low_degrees, high_degrees], axis=2).reshape(slot_count, deg_count, -1)
    coefficients = jnp.where(keep_mask[:, :, None], joined, 0.0).astype(jnp.bfloat16)
    mode_order = panel_modes[0]
    mode_degree = panel_modes[1]
    onehot = (my_orders[None, :] == mode_order[:, None]).astype(jnp.bfloat16)
    picked = jnp.take(coefficients, mode_degree, axis=1)
    local_values = jnp.einsum("ms,smc->mc", onehot, picked, preferred_element_type=jnp.float32)
    field_index = lax.axis_index("field")
    both_fields = jnp.stack(
        [
            jnp.where(field_index == 0, local_values, 0.0),
            jnp.where(field_index == 1, local_values, 0.0),
        ]
    )
    summed = lax.psum(both_fields, ("lat", "field"))
    other_field = jnp.where(field_index == 0, summed[1], summed[0]).astype(jnp.bfloat16)
    columns = other_field.astype(jnp.float32).reshape(mode_count * 2, snap_count)
    centered = (columns - jnp.mean(columns, axis=1, keepdims=True)).astype(jnp.bfloat16)
    coef_rows = coefficients.reshape(slot_count * deg_count * 2, snap_count)
    panel_values = lax.dot_general(
        coef_rows, centered, (((1,), (1,)), ((), ())), preferred_element_type=jnp.float32
    )
    panel_values = panel_values * (1.0 / (snap_count - 1))
    return panel_values.astype(jnp.bfloat16).reshape(1, slot_count, 2 * deg_count, 2 * mode_count)


def device_program(lat_count, fields_grid, basis, order_table, panel_modes):
    pairs, snap = fields_grid.shape[3], fields_grid.shape[1]
    slots, pair_total, degs = basis.shape
    modes = panel_modes.shape[1]
    first, owners = 3, lat_count // 2
    fits = (
        lat_count % 2 == 0
        and owners > first
        and modes % owners == 0
        and modes // owners == 8
        and 2 * snap == 128
        and slots == 8
        and degs <= 256
        and pair_total <= 2 * snap
        and lat_count * pairs * slots <= 512
    )
    if fits:
        return fused(lat_count, first, owners, fields_grid, basis, order_table, panel_modes)
    return local(fields_grid, basis, order_table, panel_modes)


def solution(mesh):
    placed = (P("field", None, None, "lat", None), P("lat", None, None), P(), P())
    return jax.shard_map(
        functools.partial(device_program, mesh.shape["lat"]),
        mesh=mesh, in_specs=placed, out_specs=P("field", "lat", None, None), check_vma=False,
    )
```
